128 devices in a mesh: space: 32 (over y, x, core), chan: 4 (over z).
Axes of the slice: x: 4, y: 4, z: 4, core: 2. Of those that a mesh axis runs over, the one named last changes fastest.
Arguments:
- features: bfloat16 [256, 128, 512], P('space'), may hold values from -6 to 6
- voxel_mask: int32 [256, 512], P('space'), may hold values 0 or 1
- neighbors: int32 [256, 26], P('space'), may hold values from -1 to 15, as said below
- w_conv: bfloat16 [27, 128, 128], P(None, 'chan'), may hold values from -0.109375 to 0.109375
- w_down: bfloat16 [8, 256, 128], replicated, may hold values from -0.1875 to 0.1875
- coarse_owner: int32 [256, 1], P('space'), may hold values from 0 to 31; in each aligned block of 8 rows (0 to 7, 8 to 15, ...) at most 2 rows name the same one
- cotangent: bfloat16 [2048, 256, 64], P('space', 'chan'), may hold values from -0.25 to 0.25
Outputs:
- coarse: bfloat16 [2048, 256, 64], P('space', 'chan')
- grad_conv: float32 [27, 128, 128], P(None, 'chan')
- grad_down: float32 [8, 256, 128], P(None, 'chan')
The draws below stay inside these ranges and needn't reach their ends.
Inputs may be any that keep to these rules, and one draw needn't show every extreme that they name: `neighbors`: blocks 0 to 3 of a device lie in the first x-layer of its slab and the others in the second; slabs follow each other along x in device order, and block positions in a layer lie on a 8 x 8 grid in y and z. An entry is the neighbor's slot on the own device (below 8), 8 + i for slot 4 + i of the previous device, 12 + i for slot i of the next device, or -1 where the position is empty. `coarse_owner`: among the 8 blocks of one device at most 2 name the same owner.
All inputs are finite; a program needn't handle non-finite values. No bound on the sum of `voxel_mask` on one device may be relied on, other than what follows from the above.
Results may differ from the reference program's by a relative error of at most 0.001.
The reference program's roundings to bfloat16 on the way (of `masked`, `padded`, `hidden`, `dpiece` and `dpre`) count: a program that leaves them out, or rounds other values in their place, can miss the bound.
Values may be sent and summed in bfloat16 or wider, within the bound.
A program may use at most 128 MiB of HBM per device.

```python
import math
import jax
import jax.numpy as jnp
import numpy as np
from jax import lax

C = 128
COUT = 256
E = 4
SIDE = 8
NB = 8
PEERS = 32
CAP = 2
BLOCKS = 256
SLOTS = 2048
N_SPACE = 32


OFFSETS = [(step_x, step_y, step_z) for step_x in (-1, 0, 1) for step_y in (-1, 0, 1) for step_z in (-1, 0, 1)]


def draw_neighbors(key, part):
    devices = BLOCKS // NB
    cell_count = SIDE * SIDE
    layer_keys = jax.random.split(key, devices * 2)
    orders = jax.vmap(lambda layer_key: jax.random.permutation(layer_key, cell_count))(layer_keys)
    placed = orders[:, :E].astype(jnp.int32)
    lookup = jnp.full((devices * 2, cell_count), -1, jnp.int32)
    row_ids = jnp.arange(devices * 2, dtype=jnp.int32)[:, None]
    slot_values = jnp.broadcast_to(jnp.arange(E, dtype=jnp.int32)[None, :], (devices * 2, E))
    lookup = lookup.at[row_ids, placed].set(slot_values)
    lookup = lookup.reshape(devices, 2, cell_count)
    placed = placed.reshape(devices, 2, E)
    cell_y = placed // SIDE
    cell_z = placed % SIDE
    device_ids = jnp.arange(devices, dtype=jnp.int32)[:, None, None]
    layer_ids = jnp.arange(2, dtype=jnp.int32)[None, :, None]
    columns = []
    for step_x, step_y, step_z in OFFSETS:
        if (step_x, step_y, step_z) == (0, 0, 0):
            continue
        target = layer_ids + step_x
        moved_by = jnp.where(target < 0, -1, jnp.where(target > 1, 1, 0))
        target_device = device_ids + moved_by
        target_layer = target - 2 * moved_by
        near_y = cell_y + step_y
        near_z = cell_z + step_z
        inside = (target_device >= 0) & (target_device < devices) & (near_y >= 0) & (near_y < SIDE) & (near_z >= 0) & (near_z < SIDE)
        cell_index = jnp.clip(near_y, 0, SIDE - 1) * SIDE + jnp.clip(near_z, 0, SIDE - 1)
        found_slot = lookup[jnp.clip(target_device, 0, devices - 1), target_layer, cell_index]
        slot_id = jnp.where(moved_by == 0, target_layer * E + found_slot, jnp.where(moved_by < 0, NB + found_slot, NB + E + found_slot))
        slot_id = jnp.where(inside & (found_slot >= 0), slot_id, -1)
        columns.append(jnp.broadcast_to(slot_id, (devices, 2, E)).reshape(devices * 2 * E))
    return jnp.stack(columns, axis=1).astype(jnp.int32)


def touch_ends(entries, key, least, top_value):
    index_at = [jax.random.randint(jax.random.fold_in(key, axis), (), 0, length) for axis, length in enumerate(entries.shape)]
    widest = entries.shape.index(max(entries.shape))
    beside = index_at[:widest] + [(index_at[widest] + 1) % entries.shape[widest]] + index_at[widest + 1:]
    return entries.at[tuple(index_at)].set(least).at[tuple(beside)].set(top_value)


def levels(own_key, shape, cuts, least, top_value):
    factor_of, own = 1.0, jax.random.fold_in(own_key, 6)
    for dim, blocks in cuts:
        heights = jnp.exp(jax.random.uniform(jax.random.fold_in(own, dim), (blocks,), jnp.float32, least / len(cuts), top_value / len(cuts)))
        factor_of = factor_of * jnp.repeat(heights, shape[dim] // blocks).reshape([-1 if axis == dim else 1 for axis in range(len(shape))])
    return factor_of


def assign_block(stream_key, own, number, rows, count, top, limit, lean):
    ranking = jax.random.permutation(stream_key, count)
    heavy_load, common = shares(count, rows * top, limit, lean, True), shares(count, rows * top, limit, lean, False)
    places = jnp.arange(count)

    def named(lengths, offset_by):
        used = int((lengths > 0).sum())
        fixed = max(1, used // 4)
        moved = fixed + (places - fixed + offset_by * (used - fixed)) % max(1, count - fixed)
        return jnp.zeros((count,), jnp.int32).at[ranking[jnp.where(places < fixed, places, moved)]].set(jnp.asarray(lengths, jnp.int32))

    lengths = jnp.where(number % 4 == 0, named(heavy_load, number // 4), named(common, number - number // 4 - 1))
    mixed = jax.random.permutation(jax.random.fold_in(own, 3), count)
    source_of, receiver = mixed[0:count // 2 * 2:2], mixed[1:count // 2 * 2:2]
    margin = jnp.minimum(lengths[source_of] - 1, limit - lengths[receiver]) // 2
    margin = jnp.where((source_of == ranking[0]) | (receiver == ranking[0]) | (lengths[receiver] == 0), 0, jnp.maximum(margin, 0))
    moved = jax.random.randint(jax.random.fold_in(own, 4), (count // 2,), 0, 1 << 20) % (margin + 1)
    lengths = lengths.at[source_of].add(-moved).at[receiver].add(moved)
    items = jnp.searchsorted(jnp.cumsum(lengths), jnp.arange(rows * top), side="right").astype(jnp.int32)
    table = items.reshape(top, rows).T
    table = table[jax.random.permutation(jax.random.fold_in(own, 1), rows)]
    offset_by = jax.random.randint(jax.random.fold_in(own, 2), (rows, 1), 0, top)
    return jnp.take_along_axis(table, (jnp.arange(top)[None, :] + offset_by) % top, axis=1)


def shares(count, total, most, lean, full):
    portions = [(1 << 20) // math.isqrt(grade ** lean) + 1 for grade in range(1, count + 1)]
    largest = most if full else min(most, max(-(-total // count), total * portions[0] // sum(portions)))
    least = 1 if total - largest >= count - 1 else 0
    holding, surplus = [largest] + [least] * (count - 1), total - largest - least * (count - 1)
    while surplus > 0:
        free = [i for i in range(1, count) if holding[i] < largest] or [i for i in range(1, count) if holding[i] < most]
        pool, remaining = sum([portions[i] for i in free]), surplus
        for i in free:
            more = min(most - holding[i], max(1, remaining * portions[i] // pool), surplus)
            holding[i] = holding[i] + more
            surplus = surplus - more
    return np.array(holding)


def bell_draw(key, shape, width, most, cuts=(), kind=jnp.bfloat16):
    loudness = levels(key, shape, cuts, -0.22, 0.18) if cuts else 1.0
    array = jax.random.normal(key, shape, jnp.float32) * width * loudness
    return jnp.minimum(jnp.maximum(array, -most), most).astype(kind)


def setup_inputs(seed: int = 0) -> dict:
    seeds = jax.random.split(jax.random.key(seed), 8)
    features = bell_draw(seeds[0], (BLOCKS, C, 512), 1.0, 6.0, ((0, 32),))
    voxel_mask = touch_ends((jax.random.randint(seeds[1], (BLOCKS, 512), 0, 2) < 1).astype(jnp.int32), jax.random.fold_in(seeds[1], 1), 0, 1)
    neighbors = draw_neighbors(jax.random.fold_in(seeds[7], 71), 0)
    w_conv = bell_draw(seeds[3], (27, C, C), (27 * C) ** -0.5, 0.109375, ((1, 4),))
    w_down = bell_draw(seeds[4], (8, COUT, C), (8 * C) ** -0.5, 0.1875)
    coarse_owner_keys = jax.random.split(jax.random.fold_in(seeds[5], 1), BLOCKS // NB)
    coarse_owner_turns = jax.random.permutation(jax.random.fold_in(seeds[5], 3), BLOCKS // NB)
    coarse_owner = jax.vmap(lambda own, number: assign_block(jax.random.fold_in(seeds[5], 2), own, number, NB, N_SPACE, 1, CAP, 2))(coarse_owner_keys, coarse_owner_turns).reshape((BLOCKS, 1))
    cotangent = bell_draw(seeds[6], (SLOTS, COUT, 64), (0.25 / BLOCKS ** 0.5), 0.25, ((0, 32), (1, 4)))
    return {"features": features, "voxel_mask": voxel_mask, "neighbors": neighbors, "w_conv": w_conv, "w_down": w_down, "coarse_owner": coarse_owner, "cotangent": cotangent}


OFFSETS = [(step_x, step_y, step_z) for step_x in (-1, 0, 1) for step_y in (-1, 0, 1) for step_z in (-1, 0, 1)]
CENTER = 13

def block_faces(blocks):
    block_count, channels = (blocks.shape[0], blocks.shape[1])
    cube_grid = blocks.reshape(block_count, channels, 8, 8, 8)
    face_list = [cube_grid[:, :, 0], cube_grid[:, :, 7], cube_grid[:, :, :, 0], cube_grid[:, :, :, 7], cube_grid[:, :, :, :, 0], cube_grid[:, :, :, :, 7]]
    return jnp.stack([one_face.reshape(block_count, channels, 64) for one_face in face_list], axis=1)

def neighbor_piece(lookup_rows, neighbor_ids, offset, slot_count):
    lead_axis = [which_axis for which_axis in range(3) if offset[which_axis] != 0][0]
    face_index = 2 * lead_axis + (1 if offset[lead_axis] < 0 else 0)
    row_index = jnp.where(neighbor_ids < 0, 7 * slot_count, jnp.where(neighbor_ids < slot_count, 6 * neighbor_ids + face_index, 5 * slot_count + neighbor_ids)).astype(jnp.int32)
    picked = jnp.take(lookup_rows, row_index, axis=0)
    picked = picked.reshape(picked.shape[0], picked.shape[1], 8, 8)
    other_axes = [which_axis for which_axis in range(3) if which_axis != lead_axis]
    for position_dim, which_axis in enumerate(other_axes):
        if offset[which_axis] == 1:
            picked = lax.slice_in_dim(picked, 0, 1, axis=2 + position_dim)
        elif offset[which_axis] == -1:
            picked = lax.slice_in_dim(picked, 7, 8, axis=2 + position_dim)
    return jnp.expand_dims(picked, 2 + lead_axis)

def padded_blocks(lookup_rows, neighbors, own_blocks, slot_total):
    block_count, channels = (own_blocks.shape[0], own_blocks.shape[1])
    cube_grid = own_blocks.reshape(block_count, channels, 8, 8, 8)
    planes = []
    for plane_x in range(3):
        line_list = []
        for line_y in range(3):
            cell_list = []
            for cell_z in range(3):
                position = 9 * plane_x + 3 * line_y + cell_z
                if position == CENTER:
                    cell_list.append(cube_grid)
                else:
                    column = position if position < CENTER else position - 1
                    cell_list.append(neighbor_piece(lookup_rows, neighbors[:, column], OFFSETS[position], slot_total))
            line_list.append(jnp.concatenate(cell_list, axis=4))
        planes.append(jnp.concatenate(line_list, axis=3))
    return jnp.concatenate(planes, axis=2).reshape(block_count, channels, 1000)

def window_at(padded, position):
    step_x, step_y, step_z = OFFSETS[position]
    block_count, channels = (padded.shape[0], padded.shape[1])
    cube_grid = padded.reshape(block_count, channels, 10, 10, 10)
    piece = cube_grid[:, :, 1 + step_x:9 + step_x, 1 + step_y:9 + step_y, 1 + step_z:9 + step_z]
    return piece.reshape(block_count, channels, 512)

def conv_blocks(padded, weights):
    summed = None
    for position in range(27):
        product = jnp.einsum('oi,bit->bot', weights[position].astype(jnp.float32), window_at(padded, position).astype(jnp.float32))
        summed = product if summed is None else summed + product
    return summed

def conv_weight_grad(padded, grad_out):
    spread = grad_out.astype(jnp.float32)
    grads = []
    for position in range(27):
        grads.append(jnp.einsum('bot,bit->oi', spread, window_at(padded, position).astype(jnp.float32)))
    return jnp.stack(grads)

def down_forward(weights, hidden):
    kernel = weights.reshape(2, 2, 2, weights.shape[1], weights.shape[2]).astype(jnp.float32)
    octants = hidden.reshape(hidden.shape[0], hidden.shape[1], 4, 2, 4, 2, 4, 2).astype(jnp.float32)
    result = jnp.einsum('ijkcd,bdxiyjzk->cbxyz', kernel, octants)
    return result.reshape(weights.shape[1], hidden.shape[0], 64)

def down_grad_weight(dpiece, hidden):
    grid_piece = dpiece.reshape(dpiece.shape[0], dpiece.shape[1], 4, 4, 4).astype(jnp.float32)
    octants = hidden.reshape(hidden.shape[0], hidden.shape[1], 4, 2, 4, 2, 4, 2).astype(jnp.float32)
    result = jnp.einsum('cbxyz,bdxiyjzk->ijkcd', grid_piece, octants)
    return result.reshape(8, dpiece.shape[0], hidden.shape[1])

def down_grad_input(weights, dpiece):
    kernel = weights.reshape(2, 2, 2, weights.shape[1], weights.shape[2]).astype(jnp.float32)
    grid_piece = dpiece.reshape(dpiece.shape[0], dpiece.shape[1], 4, 4, 4).astype(jnp.float32)
    result = jnp.einsum('ijkcd,cbxyz->bdxiyjzk', kernel, grid_piece)
    return result.reshape(dpiece.shape[1], weights.shape[2], 512)

def routing_table(owner, peers, capacity):
    targets = jnp.arange(peers, dtype=jnp.int32)
    dest_hits = (owner[:, None] == targets[None, :]).astype(jnp.int32)
    earlier = jnp.cumsum(dest_hits, axis=0) - dest_hits
    dest_rank = lax.optimization_barrier(jnp.sum(earlier * dest_hits, axis=1))
    places = jnp.arange(capacity, dtype=jnp.int32)
    return (owner[None, None, :] == targets[:, None, None]) & (dest_rank[None, None, :] == places[None, :, None])

def reference(features, voxel_mask, neighbors, w_conv, w_down, coarse_owner, cotangent):
    mask_float = voxel_mask.astype(jnp.float32)[:, None, :]
    masked = (features.astype(jnp.float32) * mask_float).astype(jnp.bfloat16)
    device_blocks = masked.reshape(PEERS, NB, C, 512)
    bordered = jnp.pad(device_blocks, ((1, 1), (0, 0), (0, 0), (0, 0)))
    device_neighbors = neighbors.reshape(PEERS, NB, 26)
    device_owner = coarse_owner.reshape(PEERS, NB)
    device_mask = mask_float.reshape(PEERS, NB, 1, 512)
    cotangent_grid = cotangent.reshape(PEERS, PEERS, CAP, COUT, 64)

    def one_device(device):
        own_blocks = bordered[device + 1]
        before = bordered[device][E:]
        after = bordered[device + 2][:E]
        lookup_rows = jnp.concatenate([block_faces(own_blocks).reshape(6 * NB, C, 64), block_faces(before)[:, 1], block_faces(after)[:, 0], jnp.zeros((1, C, 64), own_blocks.dtype)])
        padded = padded_blocks(lookup_rows, device_neighbors[device], own_blocks, NB)
        conv_out = conv_blocks(padded, w_conv)
        keep_mask = device_mask[device]
        pre_act = own_blocks.astype(jnp.float32) + conv_out
        hidden = (keep_mask * jax.nn.silu(pre_act)).astype(jnp.bfloat16)
        down_out = down_forward(w_down, hidden)
        chosen = routing_table(device_owner[device], PEERS, CAP).astype(jnp.float32)
        pieces = lax.optimization_barrier(down_out.astype(jnp.bfloat16)).astype(jnp.float32)
        outgoing = jnp.einsum('drj,cjq->drcq', chosen, pieces).astype(jnp.bfloat16)
        returned = cotangent_grid[:, device].astype(jnp.float32)
        dpiece = jnp.einsum('drj,drcq->cjq', chosen, returned).astype(jnp.bfloat16)
        down_grad = down_grad_weight(dpiece, hidden)
        dhidden = down_grad_input(w_down, dpiece)
        sigmoid = jax.nn.sigmoid(pre_act)
        dpre = (dhidden * keep_mask * sigmoid * (1.0 + pre_act * (1.0 - sigmoid))).astype(jnp.bfloat16)
        conv_grad = conv_weight_grad(padded, dpre)
        return (outgoing, conv_grad, down_grad)
    outgoing, conv_grads, down_grads = lax.map(one_device, jnp.arange(PEERS, dtype=jnp.int32))
    coarse = jnp.transpose(outgoing, (1, 0, 2, 3, 4)).reshape(SLOTS, COUT, 64)
    return (coarse, lax.optimization_barrier(jnp.sum(conv_grads, axis=0)), lax.optimization_barrier(jnp.sum(down_grads, axis=0)))
```

```python
import jax
import jax.numpy as jnp
from jax import lax
from jax.experimental import pallas as pl
from jax.experimental.pallas import tpu as pltpu
from jax.sharding import PartitionSpec as P

F32 = jnp.float32
BF16 = jnp.bfloat16
NT = (((1,), (1,)), ((), ()))
ZERO_PLANE = 72


def voxel_order():
    row = lax.broadcasted_iota(jnp.int32, (256, 256), 0)
    col = lax.broadcasted_iota(jnp.int32, (256, 256), 1)
    y = ((row >> 2) & 3) * 2 + ((row >> 5) & 1)
    z = (row & 3) * 2 + ((row >> 4) & 1)
    source = (row & ~63) + y * 8 + z
    return (source == col).astype(F32).astype(BF16)


def planes_kernel(features, mask, planes, row_mask):
    order = voxel_order()
    mine = lax.axis_index("chan") * 2

    @pl.loop(0, 8)
    def _(g):
        keep = mask[pl.ds(g, 1), :].astype(F32).astype(BF16)
        masked = features[g] * keep
        for h in range(2):
            turned = lax.dot_general(
                order, masked[:, 256 * h : 256 * h + 256], NT, preferred_element_type=F32
            )
            planes[pl.ds(8 * g + 4 * h, 4)] = turned.astype(BF16).reshape(4, 64, 128)

    for b in range(2):
        keep = mask[pl.ds(mine + b, 1), :].astype(F32)
        for h in range(2):
            wide = jnp.broadcast_to(keep[:, 256 * h : 256 * h + 256], (128, 256)).astype(BF16)
            turned = lax.dot_general(order, wide, NT, preferred_element_type=F32)
            row_mask[b, 256 * h : 256 * h + 256, :] = turned


def make_planes(features, mask):
    return pl.pallas_call(
        planes_kernel,
        out_shape=(
            jax.ShapeDtypeStruct((64, 64, 128), BF16),
            jax.ShapeDtypeStruct((2, 512, 128), F32),
        ),
    )(features, mask)


def fill_plane(windows, planes, near, b, mine, xp, sx):
    local_x = lax.rem(xp + 7, 8)
    qy = (lax.broadcasted_iota(jnp.int32, (16, 128), 0) >> 2) & 3
    qz = lax.broadcasted_iota(jnp.int32, (16, 128), 0) & 3
    loaded = {}
    for sy in (-1, 0, 1):
        for sz in (-1, 0, 1):
            position = 9 * (sx + 1) + 3 * (sy + 1) + (sz + 1)
            if position == 13:
                slot = mine + b
            else:
                slot = near[mine + b, position if position < 13 else position - 1]
            plane = jnp.where(
                slot < 0, ZERO_PLANE, jnp.where(slot < 8, 8 * slot + local_x, 56 + slot)
            )
            loaded[sy, sz] = planes[plane].astype(F32).reshape(4, 16, 128)

    def merged(oy, sz, tile):
        inner = loaded[0, sz][tile]
        if oy == 0:
            return inner
        return jnp.where(qy == (3 if oy < 0 else 0), loaded[oy, sz][tile], inner)

    def turned(value, shift):
        return value if shift % 16 == 0 else pltpu.roll(value, shift % 16, 0)

    for i in range(4):
        for j in range(4):
            oy = (-1, 0, 0, 1)[i]
            oz = (-1, 0, 0, 1)[j]
            tile = (1, 0, 1, 0)[i] * 2 + (1, 0, 1, 0)[j]
            value = turned(merged(oy, 0, tile), -4 * oy - oz)
            if oz != 0:
                edge = turned(merged(oy, oz, tile), -4 * oy + 3 * oz)
                value = jnp.where(qz == (0 if oz < 0 else 3), edge, value)
            value = value.astype(BF16)
            for p in range(2):
                for e in range(2):
                    dy, dz = i - p, j - e
                    if 0 <= dy <= 2 and 0 <= dz <= 2:
                        row = 32 * p + 16 * e
                        col = 128 * (3 * dy + dz)
                        windows[b, xp, row : row + 16, col : col + 128] = value


def block_kernel(
    near, planes, before, after, row_mask, w_conv, w_down, dpiece,
    pieces, conv_grad, down_grad,
    table, windows, octants, factor, slopes,
):
    mine = lax.axis_index("chan") * 2
    table[0:64] = planes[...]
    table[64:68] = before[...]
    table[68:72] = after[...]
    table[72] = jnp.zeros((64, 128), BF16)
    for b in range(2):
        fill_plane(windows, table, near, b, mine, 0, -1)
        fill_plane(windows, table, near, b, mine, 9, 1)

        @pl.loop(1, 9)
        def _(xp):
            fill_plane(windows, table, near, b, mine, xp, 0)

    for b in range(2):
        total = None
        for dx in range(3):
            part = lax.dot_general(
                windows[b, dx : dx + 8].reshape(512, 1152), w_conv[dx], NT,
                preferred_element_type=F32,
            )
            total = part if total is None else total + part
        own = table[pl.ds(8 * (mine + b), 8)].astype(F32).reshape(512, 128)
        pre = own + total
        keep = row_mask[b]
        gate = jax.nn.sigmoid(pre)
        hidden = (keep * (pre * gate)).astype(BF16).reshape(4, 2, 4, 16, 128)
        factor[b] = keep * gate * (1.0 + pre * (1.0 - gate))
        for a in range(2):
            for t in range(4):
                octants[4 * a + t, 64 * b : 64 * b + 64, :] = hidden[:, a, t].reshape(64, 128)
    total = None
    for o in range(8):
        part = lax.dot_general(w_down[o], octants[o], NT, preferred_element_type=F32)
        total = part if total is None else total + part
    pieces[...] = total.astype(BF16)

    piece = dpiece[...]
    piece_rows = piece.astype(F32).T.astype(BF16)
    for o in range(8):
        down_grad[o] = jnp.dot(piece, octants[o], preferred_element_type=F32)
    for b in range(2):
        for a in range(2):
            for t in range(4):
                o = 4 * a + t
                dhidden = jnp.dot(
                    piece_rows[64 * b : 64 * b + 64], w_down[o], preferred_element_type=F32
                ).reshape(4, 16, 128)
                for qx in range(4):
                    row = 64 * (2 * qx + a) + 16 * t
                    slopes[b, row : row + 16, :] = dhidden[qx] * factor[b, row : row + 16, :]
    for dx in range(3):
        total = None
        for b in range(2):
            rows = slopes[b].astype(BF16).astype(F32).T.astype(BF16)
            part = jnp.dot(
                rows, windows[b, dx : dx + 8].reshape(512, 1152), preferred_element_type=F32
            )
            total = part if total is None else total + part
        conv_grad[dx] = total


def run_blocks(near, planes, before, after, row_mask, w_conv, w_down, dpiece):
    vmem = pl.BlockSpec(memory_space=pltpu.VMEM)
    return pl.pallas_call(
        block_kernel,
        out_shape=(
            jax.ShapeDtypeStruct((256, 128), BF16),
            jax.ShapeDtypeStruct((3, 128, 1152), F32),
            jax.ShapeDtypeStruct((8, 256, 128), F32),
        ),
        in_specs=[pl.BlockSpec(memory_space=pltpu.SMEM)] + [vmem] * 7,
        out_specs=(vmem, vmem, vmem),
        scratch_shapes=[
            pltpu.VMEM((73, 64, 128), BF16),
            pltpu.VMEM((2, 10, 64, 1152), BF16),
            pltpu.VMEM((8, 128, 128), BF16),
            pltpu.VMEM((2, 512, 128), F32),
            pltpu.VMEM((2, 512, 128), F32),
        ],
        compiler_params=pltpu.CompilerParams(vmem_limit_bytes=56 << 20),
    )(near, planes, before, after, row_mask, w_conv, w_down, dpiece)


def routing_table(owner, peers, capacity):
    targets = jnp.arange(peers, dtype=jnp.int32)
    dest_hits = (owner[:, None] == targets[None, :]).astype(jnp.int32)
    earlier = jnp.cumsum(dest_hits, axis=0) - dest_hits
    dest_rank = jnp.sum(earlier * dest_hits, axis=1)
    places = jnp.arange(capacity, dtype=jnp.int32)
    return (owner[None, None, :] == targets[:, None, None]) & (
        dest_rank[None, None, :] == places[None, :, None]
    )


def local(features, voxel_mask, neighbors, w_conv, w_down, coarse_owner, cotangent):
    peers = lax.axis_size("space")
    shards = lax.axis_size("chan")
    planes, row_mask = make_planes(features, voxel_mask)
    by_block = planes.reshape(8, 8, 64, 128)
    before = lax.ppermute(by_block[4:, 7], "space", [(i, i + 1) for i in range(peers - 1)])
    after = lax.ppermute(by_block[:4, 0], "space", [(i + 1, i) for i in range(peers - 1)])
    w_rows = w_conv.reshape(3, 9, -1, 128).transpose(0, 2, 1, 3).reshape(3, -1, 1152)
    w_all = lax.all_gather(w_rows, "chan", axis=1, tiled=True)
    capacity = cotangent.shape[0] // peers
    down_width = cotangent.shape[1]
    chosen = routing_table(coarse_owner[:, 0], peers, capacity).astype(BF16)
    returned = lax.all_to_all(
        cotangent.reshape(peers, capacity, down_width, 64),
        "space", split_axis=0, concat_axis=0, tiled=True,
    )
    dpiece = jnp.einsum(
        "drj,drcq->jcq", chosen, returned, preferred_element_type=F32
    ).astype(BF16)
    dpiece = dpiece.reshape(shards, 2, down_width, 64).transpose(0, 2, 1, 3)
    dpiece = lax.all_to_all(dpiece, "chan", split_axis=0, concat_axis=0, tiled=True)
    dpiece = dpiece.reshape(shards * down_width, 128)
    pieces, conv_grad, down_grad = run_blocks(
        neighbors, planes, before, after, row_mask, w_all, w_down, dpiece
    )
    pieces = lax.all_to_all(
        pieces.reshape(shards, down_width, 128), "chan", split_axis=0, concat_axis=0, tiled=True
    )
    pieces = pieces.reshape(shards, down_width, 2, 64).transpose(0, 2, 1, 3)
    pieces = pieces.reshape(8, down_width, 64)
    outgoing = jnp.einsum(
        "drj,jcq->drcq", chosen, pieces, preferred_element_type=F32
    ).astype(BF16)
    arrived = lax.all_to_all(outgoing, "space", split_axis=0, concat_axis=0, tiled=True)
    coarse = arrived.reshape(peers * capacity, down_width, 64)
    conv_part = lax.psum_scatter(conv_grad, "chan", scatter_dimension=1, tiled=True)
    down_part = lax.psum_scatter(down_grad, "chan", scatter_dimension=1, tiled=True)
    conv_sum, down_sum = lax.psum((conv_part, down_part), "space")
    conv_sum = conv_sum.reshape(3, -1, 9, 128).transpose(0, 2, 1, 3).reshape(27, -1, 128)
    return (coarse, conv_sum, down_sum)


def solution(mesh):
    in_specs = (
        P("space", None, None),
        P("space", None),
        P("space", None),
        P(None, "chan", None),
        P(),
        P("space", None),
        P("space", "chan", None),
    )
    out_specs = (P("space", "chan", None), P(None, "chan", None), P(None, "chan", None))
    return jax.shard_map(local, mesh=mesh, in_specs=in_specs, out_specs=out_specs, check_vma=False)
```

```python
import jax
import jax.numpy as jnp
from jax import lax
from jax.experimental import pallas as pl
from jax.experimental.pallas import tpu as pltpu
from jax.sharding import PartitionSpec as P

F32 = jnp.float32
BF16 = jnp.bfloat16
NT = (((1,), (1,)), ((), ()))
ZERO_PLANE = 72


def voxel_order():
    row = lax.broadcasted_iota(jnp.int32, (256, 256), 0)
    col = lax.broadcasted_iota(jnp.int32, (256, 256), 1)
    y = ((row >> 2) & 3) * 2 + ((row >> 5) & 1)
    z = (row & 3) * 2 + ((row >> 4) & 1)
    source = (row & ~63) + y * 8 + z
    return (source == col).astype(F32).astype(BF16)


def planes_kernel(features, mask, planes, row_mask):
    order = voxel_order()
    mine = lax.axis_index("chan") * 2

    @pl.loop(0, 8)
    def _(g):
        keep = mask[pl.ds(g, 1), :].astype(F32).astype(BF16)
        masked = features[g] * keep
        for h in range(2):
            turned = lax.dot_general(
                order, masked[:, 256 * h : 256 * h + 256], NT, preferred_element_type=F32
            )
            planes[pl.ds(8 * g + 4 * h, 4)] = turned.astype(BF16).reshape(4, 64, 128)

    for b in range(2):
        keep = mask[pl.ds(mine + b, 1), :].astype(F32)
        for h in range(2):
            wide = jnp.broadcast_to(keep[:, 256 * h : 256 * h + 256], (128, 256)).astype(BF16)
            turned = lax.dot_general(order, wide, NT, preferred_element_type=F32)
            row_mask[b, 256 * h : 256 * h + 256, :] = turned


def make_planes(features, mask):
    return pl.pallas_call(
        planes_kernel,
        out_shape=(
            jax.ShapeDtypeStruct((64, 64, 128), BF16),
            jax.ShapeDtypeStruct((2, 512, 128), F32),
        ),
    )(features, mask)


def fill_plane(windows, planes, near, b, mine, xp, sx):
    local_x = lax.rem(xp + 7, 8)
    qy = (lax.broadcasted_iota(jnp.int32, (16, 128), 0) >> 2) & 3
    qz = lax.broadcasted_iota(jnp.int32, (16, 128), 0) & 3
    loaded = {}
    for sy in (-1, 0, 1):
        for sz in (-1, 0, 1):
            position = 9 * (sx + 1) + 3 * (sy + 1) + (sz + 1)
            if position == 13:
                slot = mine + b
            else:
                slot = near[mine + b, position if position < 13 else position - 1]
            plane = jnp.where(
                slot < 0, ZERO_PLANE, jnp.where(slot < 8, 8 * slot + local_x, 56 + slot)
            )
            loaded[sy, sz] = planes[plane].astype(F32).reshape(4, 16, 128)

    def merged(oy, sz, tile):
        inner = loaded[0, sz][tile]
        if oy == 0:
            return inner
        return jnp.where(qy == (3 if oy < 0 else 0), loaded[oy, sz][tile], inner)

    def turned(value, shift):
        return value if shift % 16 == 0 else pltpu.roll(value, shift % 16, 0)

    for i in range(4):
        for j in range(4):
            oy = (-1, 0, 0, 1)[i]
            oz = (-1, 0, 0, 1)[j]
            tile = (1, 0, 1, 0)[i] * 2 + (1, 0, 1, 0)[j]
            value = turned(merged(oy, 0, tile), -4 * oy - oz)
            if oz != 0:
                edge = turned(merged(oy, oz, tile), -4 * oy + 3 * oz)
                value = jnp.where(qz == (0 if oz < 0 else 3), edge, value)
            value = value.astype(BF16)
            for p in range(2):
                for e in range(2):
                    dy, dz = i - p, j - e
                    if 0 <= dy <= 2 and 0 <= dz <= 2:
                        row = 32 * p + 16 * e
                        col = 128 * (3 * dy + dz)
                        windows[b, xp, row : row + 16, col : col + 128] = value


def grid_of(peers):
    chips = peers // 2
    across = 4 if chips == 16 else (2 if chips == 4 else 1)
    return chips // across, across


class Links:
    def __init__(self):
        self.ny, self.nx = grid_of(lax.axis_size("space"))
        self.nz = lax.axis_size("chan")
        space = lax.axis_index("space")
        self.space = space
        self.z = lax.axis_index("chan")
        self.core = lax.rem(space, 2)
        self.x = lax.rem(space // 2, self.nx)
        self.y = space // (2 * self.nx)

    def device(self, y=None, x=None, z=None, core=None):
        y = self.y if y is None else y
        x = self.x if x is None else x
        z = self.z if z is None else z
        core = self.core if core is None else core
        return ((y * self.nx + x) * 2 + core, z)


def send(source, target, sems, device):
    pltpu.make_async_remote_copy(
        src_ref=source, dst_ref=target, send_sem=sems[0], recv_sem=sems[1],
        device_id=device, device_id_type=pl.DeviceIdType.MESH,
    ).start()


def arrived(ref, sems, device):
    pltpu.make_async_remote_copy(
        src_ref=ref, dst_ref=ref, send_sem=sems[0], recv_sem=sems[1],
        device_id=device, device_id_type=pl.DeviceIdType.MESH,
    ).wait_recv()


def left(ref, sems, device):
    pltpu.make_async_remote_copy(
        src_ref=ref, dst_ref=ref, send_sem=sems[0], recv_sem=sems[1],
        device_id=device, device_id_type=pl.DeviceIdType.MESH,
    ).wait_send()


def shifted(place, step, count):
    return lax.rem(place + step, count)


class Reduce:
    def __init__(self, links, grads, pair, first, rest, second, sums, sems):
        self.k = links
        self.grads, self.pair, self.first, self.rest = grads, pair, first, rest
        self.second, self.sums, self.sems = second, sums, sems
        self.partner = links.device(core=1 - links.core)
        k = links
        self.major = [("z", k.nz), ("x", k.nx), ("y", k.ny)]
        self.minor = [
            (("y", k.ny), ("x", k.nx)), (("z", k.nz), ("y", k.ny)), (("z", k.nz), ("x", k.nx)),
        ]
        self.cell = 256 // (k.nx * k.ny)

    def at(self, name):
        return getattr(self.k, name)

    def sem(self, phase, color):
        return (self.sems.at[0, phase, color], self.sems.at[1, phase, color])

    def start_pair(self, color):
        away = pl.multiple_of(256 * (1 - self.k.core), 256)
        send(
            self.grads.at[color, :, pl.ds(away, 256)], self.pair.at[color],
            self.sem(0, color), self.partner,
        )

    def part(self, color, place):
        half = 256 * self.k.core
        if color == 0:
            return self.grads.at[color, place, pl.ds(pl.multiple_of(half, 256), 256)]
        rows = 256 // self.major[color][1]
        return self.grads.at[color, :, pl.ds(pl.multiple_of(half + place * rows, rows), rows)]

    def start_major(self, color):
        half = pl.ds(pl.multiple_of(256 * self.k.core, 256), 256)
        arrived(self.pair.at[color], self.sem(0, color), self.partner)
        for z in range(self.k.nz):
            self.grads[color, z, half] += self.pair[color, z]
        name, count = self.major[color]
        for step in range(1, count):
            place = shifted(self.at(name), step, count)
            send(
                self.part(color, place), self.first[color].at[step - 1],
                self.sem(1, color), self.k.device(**{name: place}),
            )

    def start_minor(self, color):
        name, count = self.major[color]
        place = self.at(name)
        if count > 1:
            arrived(self.first[color].at[0 : count - 1], self.sem(1, color), self.partner)
        half = 256 * self.k.core
        if color == 0:
            total = self.grads[0, place, pl.ds(pl.multiple_of(half, 256), 256)]
        else:
            rows = 256 // count
            total = self.grads[color, :, pl.ds(pl.multiple_of(half + place * rows, rows), rows)]
        for step in range(count - 1):
            total = total + self.first[color][step]
        (n0, c0), (n1, c1) = self.minor[color]
        self.rest[color][...] = total.reshape(c0, c1, self.cell, 128)
        for step0 in range(c0):
            for step1 in range(c1):
                if step0 == 0 and step1 == 0:
                    continue
                p0 = shifted(self.at(n0), step0, c0)
                p1 = shifted(self.at(n1), step1, c1)
                send(
                    self.rest[color].at[p0, p1], self.second[color].at[step0 * c1 + step1 - 1],
                    self.sem(2, color), self.k.device(**{n0: p0, n1: p1}),
                )

    def home(self, color):
        k = self.k
        inner = (k.x * k.ny + k.y) if color == 1 else (k.y * k.nx + k.x)
        return pl.ds(pl.multiple_of(256 * k.core + inner * self.cell, self.cell), self.cell)

    def start_spread(self, color):
        k = self.k
        (n0, c0), (n1, c1) = self.minor[color]
        if c0 * c1 > 1:
            arrived(self.second[color], self.sem(2, color), self.partner)
        total = self.rest[color][self.at(n0), self.at(n1)]
        for step in range(c0 * c1 - 1):
            total = total + self.second[color][step]
        self.sums[color, self.home(color)] = total
        for step0 in range(k.ny):
            for step1 in range(k.nx):
                if step0 == 0 and step1 == 0:
                    continue
                y = shifted(k.y, step0, k.ny)
                x = shifted(k.x, step1, k.nx)
                mine = self.sums.at[color, self.home(color)]
                send(mine, mine, self.sem(3, color), k.device(y=y, x=x))

    def start_share(self, color):
        k = self.k
        others = k.nx * k.ny - 1
        if others:
            arrived(self.sums.at[color, 0 : others * self.cell], self.sem(3, color), self.partner)
        half = pl.ds(pl.multiple_of(256 * k.core, 256), 256)
        mine = self.sums.at[color, half]
        send(mine, mine, self.sem(4, color), self.partner)

    def finish(self, color):
        k = self.k
        arrived(self.sums.at[color, 0:256], self.sem(4, color), self.partner)
        left(self.pair.at[color], self.sem(0, color), self.partner)
        count = self.major[color][1]
        if count > 1:
            left(self.first[color].at[0 : count - 1], self.sem(1, color), self.partner)
        if self.minor[color][0][1] * self.minor[color][1][1] > 1:
            left(self.second[color], self.sem(2, color), self.partner)
        others = k.nx * k.ny - 1
        if others:
            left(self.sums.at[color, 0 : others * self.cell], self.sem(3, color), self.partner)
        left(self.sums.at[color, 0:256], self.sem(4, color), self.partner)


def reduce_scratch(peers, nz):
    ny, nx = grid_of(peers)
    cell = 256 // (nx * ny)
    return [
        pltpu.VMEM((3, nz, 512, 128), F32),
        pltpu.VMEM((3, nz, 256, 128), F32),
        pltpu.VMEM((nz - 1, 256, 128), F32),
        pltpu.VMEM((max(nx - 1, 1), nz, 256 // nx, 128), F32),
        pltpu.VMEM((max(ny - 1, 1), nz, 256 // ny, 128), F32),
        pltpu.VMEM((ny, nx, cell, 128), F32),
        pltpu.VMEM((nz, ny, cell, 128), F32),
        pltpu.VMEM((nz, nx, cell, 128), F32),
        pltpu.VMEM((max(ny * nx - 1, 1), cell, 128), F32),
        pltpu.VMEM((nz * ny - 1, cell, 128), F32),
        pltpu.VMEM((nz * nx - 1, cell, 128), F32),
        pltpu.VMEM((3, 512, 128), F32),
        pltpu.SemaphoreType.DMA((2, 5, 3)),
    ]


def enter(links):
    barrier = pltpu.get_barrier_semaphore()
    k = links
    count = 0
    for step in range(1, k.nz):
        z = shifted(k.z, step, k.nz)
        for other in range(k.ny):
            y = shifted(k.y, other, k.ny)
            pl.semaphore_signal(
                barrier, inc=1, device_id=k.device(y=y, z=z), device_id_type=pl.DeviceIdType.MESH
            )
            count += 1
        for other in range(1, k.nx):
            x = shifted(k.x, other, k.nx)
            pl.semaphore_signal(
                barrier, inc=1, device_id=k.device(x=x, z=z), device_id_type=pl.DeviceIdType.MESH
            )
            count += 1
    for step in range(1, k.ny * k.nx * 2):
        space = shifted(k.space, step, k.ny * k.nx * 2)
        pl.semaphore_signal(
            barrier, inc=1, device_id=(space, k.z), device_id_type=pl.DeviceIdType.MESH
        )
        count += 1
    pl.semaphore_wait(barrier, count)


def block_kernel(
    near, planes, before, after, row_mask, w_conv, w_down, dpiece,
    pieces, conv_sum, down_sum,
    table, windows, octants, factor, slopes,
    grads, pair, first_z, first_x, first_y, rest_0, rest_1, rest_2,
    second_0, second_1, second_2, sums, sems,
):
    links = Links()
    reduce = Reduce(
        links, grads, pair, (first_z, first_x, first_y), (rest_0, rest_1, rest_2),
        (second_0, second_1, second_2), sums, sems,
    )
    enter(links)
    mine = lax.axis_index("chan") * 2
    table[0:64] = planes[...]
    table[64:68] = before[...]
    table[68:72] = after[...]
    table[72] = jnp.zeros((64, 128), BF16)
    for z in range(4):
        grads[1, z, 448:512] = jnp.zeros((64, 128), F32)
        grads[2, z, 416:512] = jnp.zeros((96, 128), F32)
    for b in range(2):
        fill_plane(windows, table, near, b, mine, 0, -1)
        fill_plane(windows, table, near, b, mine, 9, 1)

        @pl.loop(1, 9)
        def _(xp):
            fill_plane(windows, table, near, b, mine, xp, 0)

    for b in range(2):
        total = None
        for dx in range(3):
            part = lax.dot_general(
                windows[b, dx : dx + 8].reshape(512, 1152), w_conv[dx], NT,
                preferred_element_type=F32,
            )
            total = part if total is None else total + part
        own = table[pl.ds(8 * (mine + b), 8)].astype(F32).reshape(512, 128)
        pre = own + total
        keep = row_mask[b]
        gate = jax.nn.sigmoid(pre)
        hidden = (keep * (pre * gate)).astype(BF16).reshape(4, 2, 4, 16, 128)
        factor[b] = keep * gate * (1.0 + pre * (1.0 - gate))
        for a in range(2):
            for t in range(4):
                octants[4 * a + t, 64 * b : 64 * b + 64, :] = hidden[:, a, t].reshape(64, 128)
    total = None
    for o in range(8):
        part = lax.dot_general(w_down[o], octants[o], NT, preferred_element_type=F32)
        total = part if total is None else total + part
    pieces[...] = total.astype(BF16)

    piece = dpiece[...]
    piece_rows = piece.astype(F32).T.astype(BF16)
    for o in range(8):
        part = jnp.dot(piece, octants[o], preferred_element_type=F32)
        for z in range(4):
            grads[0, z, 64 * o : 64 * o + 64, :] = part[64 * z : 64 * z + 64]
    reduce.start_pair(0)
    for b in range(2):
        for a in range(2):
            for t in range(4):
                o = 4 * a + t
                dhidden = jnp.dot(
                    piece_rows[64 * b : 64 * b + 64], w_down[o], preferred_element_type=F32
                ).reshape(4, 16, 128)
                for qx in range(4):
                    row = 64 * (2 * qx + a) + 16 * t
                    slopes[b, row : row + 16, :] = dhidden[qx] * factor[b, row : row + 16, :]
    for dx in range(3):
        total = None
        for b in range(2):
            rows = slopes[b].astype(BF16).astype(F32).T.astype(BF16)
            part = jnp.dot(
                rows, windows[b, dx : dx + 8].reshape(512, 1152), preferred_element_type=F32
            )
            total = part if total is None else total + part
        for d in range(9):
            k = 9 * dx + d
            color, row = (1, 32 * k) if k < 14 else (2, 32 * (k - 14))
            for z in range(4):
                grads[color, z, row : row + 32, :] = total[
                    32 * z : 32 * z + 32, 128 * d : 128 * d + 128
                ]
        if dx == 0:
            reduce.start_major(0)
        else:
            reduce.start_pair(dx)
    reduce.start_major(1)
    reduce.start_major(2)
    for color in range(3):
        reduce.start_minor(color)
    for color in range(3):
        reduce.start_spread(color)
    for color in range(3):
        reduce.start_share(color)
    for color in range(3):
        reduce.finish(color)
    for o in range(8):
        down_sum[o] = sums[0, 64 * o : 64 * o + 64]
    for k in range(27):
        color, row = (1, 32 * k) if k < 14 else (2, 32 * (k - 14))
        conv_sum[k] = sums[color, row : row + 32]


def run_blocks(near, planes, before, after, row_mask, w_conv, w_down, dpiece):
    vmem = pl.BlockSpec(memory_space=pltpu.VMEM)
    return pl.pallas_call(
        block_kernel,
        out_shape=(
            jax.ShapeDtypeStruct((256, 128), BF16),
            jax.ShapeDtypeStruct((27, 32, 128), F32),
            jax.ShapeDtypeStruct((8, 64, 128), F32),
        ),
        in_specs=[pl.BlockSpec(memory_space=pltpu.SMEM)] + [vmem] * 7,
        out_specs=(vmem, vmem, vmem),
        scratch_shapes=[
            pltpu.VMEM((73, 64, 128), BF16),
            pltpu.VMEM((2, 10, 64, 1152), BF16),
            pltpu.VMEM((8, 128, 128), BF16),
            pltpu.VMEM((2, 512, 128), F32),
            pltpu.VMEM((2, 512, 128), F32),
        ]
        + reduce_scratch(lax.axis_size("space"), lax.axis_size("chan")),
        compiler_params=pltpu.CompilerParams(
            vmem_limit_bytes=56 << 20, collective_id=0, has_side_effects=True
        ),
    )(near, planes, before, after, row_mask, w_conv, w_down, dpiece)


def routing_table(owner, peers, capacity):
    targets = jnp.arange(peers, dtype=jnp.int32)
    dest_hits = (owner[:, None] == targets[None, :]).astype(jnp.int32)
    earlier = jnp.cumsum(dest_hits, axis=0) - dest_hits
    dest_rank = jnp.sum(earlier * dest_hits, axis=1)
    places = jnp.arange(capacity, dtype=jnp.int32)
    return (owner[None, None, :] == targets[:, None, None]) & (
        dest_rank[None, None, :] == places[None, :, None]
    )


def local(features, voxel_mask, neighbors, w_conv, w_down, coarse_owner, cotangent):
    peers = lax.axis_size("space")
    shards = lax.axis_size("chan")
    planes, row_mask = make_planes(features, voxel_mask)
    by_block = planes.reshape(8, 8, 64, 128)
    before = lax.ppermute(by_block[4:, 7], "space", [(i, i + 1) for i in range(peers - 1)])
    after = lax.ppermute(by_block[:4, 0], "space", [(i + 1, i) for i in range(peers - 1)])
    w_rows = w_conv.reshape(3, 9, -1, 128).transpose(0, 2, 1, 3).reshape(3, -1, 1152)
    w_all = lax.all_gather(w_rows, "chan", axis=1, tiled=True)
    capacity = cotangent.shape[0] // peers
    down_width = cotangent.shape[1]
    chosen = routing_table(coarse_owner[:, 0], peers, capacity).astype(BF16)
    returned = lax.all_to_all(
        cotangent.reshape(peers, capacity, down_width, 64),
        "space", split_axis=0, concat_axis=0, tiled=True,
    )
    dpiece = jnp.einsum(
        "drj,drcq->jcq", chosen, returned, preferred_element_type=F32
    ).astype(BF16)
    dpiece = dpiece.reshape(shards, 2, down_width, 64).transpose(0, 2, 1, 3)
    dpiece = lax.all_to_all(dpiece, "chan", split_axis=0, concat_axis=0, tiled=True)
    dpiece = dpiece.reshape(shards * down_width, 128)
    pieces, conv_sum, down_sum = run_blocks(
        neighbors, planes, before, after, row_mask, w_all, w_down, dpiece
    )
    pieces = lax.all_to_all(
        pieces.reshape(shards, down_width, 128), "chan", split_axis=0, concat_axis=0, tiled=True
    )
    pieces = pieces.reshape(shards, down_width, 2, 64).transpose(0, 2, 1, 3)
    pieces = pieces.reshape(8, down_width, 64)
    outgoing = jnp.einsum(
        "drj,jcq->drcq", chosen, pieces, preferred_element_type=F32
    ).astype(BF16)
    arrived = lax.all_to_all(outgoing, "space", split_axis=0, concat_axis=0, tiled=True)
    coarse = arrived.reshape(peers * capacity, down_width, 64)
    return (coarse, conv_sum, down_sum)


def solution(mesh):
    in_specs = (
        P("space", None, None),
        P("space", None),
        P("space", None),
        P(None, "chan", None),
        P(),
        P("space", None),
        P("space", "chan", None),
    )
    out_specs = (P("space", "chan", None), P(None, "chan", None), P(None, "chan", None))
    return jax.shard_map(local, mesh=mesh, in_specs=in_specs, out_specs=out_specs, check_vma=False)
```

```python
import jax
import jax.numpy as jnp
from jax import lax
from jax.experimental import pallas as pl
from jax.experimental.pallas import tpu as pltpu
from jax.sharding import PartitionSpec as P

F32 = jnp.float32
BF16 = jnp.bfloat16
NT = (((1,), (1,)), ((), ()))


def voxel_order():
    row = lax.broadcasted_iota(jnp.int32, (256, 256), 0)
    col = lax.broadcasted_iota(jnp.int32, (256, 256), 1)
    y = ((row >> 2) & 3) * 2 + ((row >> 5) & 1)
    z = (row & 3) * 2 + ((row >> 4) & 1)
    source = (row & ~63) + y * 8 + z
    return (source == col).astype(F32).astype(BF16)


def fill_plane(windows, planes, near, b, mine, xp, sx):
    qy = (lax.broadcasted_iota(jnp.int32, (16, 128), 0) >> 2) & 3
    qz = lax.broadcasted_iota(jnp.int32, (16, 128), 0) & 3
    loaded = {}
    for sy in (-1, 0, 1):
        for sz in (-1, 0, 1):
            position = 9 * (sx + 1) + 3 * (sy + 1) + (sz + 1)
            if position == 13:
                slot = mine + b
            else:
                slot = near[mine + b, position if position < 13 else position - 1]
            if sx == 0:
                plane = jnp.where((slot < 0) | (slot > 7), 64, 8 * slot + xp - 1)
            else:
                plane = jnp.where(slot < 0, 16, slot)
            loaded[sy, sz] = planes[plane].astype(F32).reshape(4, 16, 128)

    def merged(oy, sz, tile):
        inner = loaded[0, sz][tile]
        if oy == 0:
            return inner
        return jnp.where(qy == (3 if oy < 0 else 0), loaded[oy, sz][tile], inner)

    def turned(value, shift):
        return value if shift % 16 == 0 else pltpu.roll(value, shift % 16, 0)

    for i in range(4):
        for j in range(4):
            oy = (-1, 0, 0, 1)[i]
            oz = (-1, 0, 0, 1)[j]
            tile = (1, 0, 1, 0)[i] * 2 + (1, 0, 1, 0)[j]
            value = turned(merged(oy, 0, tile), -4 * oy - oz)
            if oz != 0:
                edge = turned(merged(oy, oz, tile), -4 * oy + 3 * oz)
                value = jnp.where(qz == (0 if oz < 0 else 3), edge, value)
            value = value.astype(BF16)
            for p in range(2):
                for e in range(2):
                    dy, dz = i - p, j - e
                    if 0 <= dy <= 2 and 0 <= dz <= 2:
                        row = 32 * p + 16 * e
                        col = 128 * (3 * dy + dz)
                        windows[b, xp, row : row + 16, col : col + 128] = value


def grid_of(peers):
    chips = peers // 2
    across = 4 if chips == 16 else (2 if chips == 4 else 1)
    return chips // across, across


class Links:
    def __init__(self):
        self.ny, self.nx = grid_of(lax.axis_size("space"))
        self.nz = lax.axis_size("chan")
        space = lax.axis_index("space")
        self.space = space
        self.z = lax.axis_index("chan")
        self.core = lax.rem(space, 2)
        self.x = lax.rem(space // 2, self.nx)
        self.y = space // (2 * self.nx)

    def device(self, y=None, x=None, z=None, core=None):
        y = self.y if y is None else y
        x = self.x if x is None else x
        z = self.z if z is None else z
        core = self.core if core is None else core
        return ((y * self.nx + x) * 2 + core, z)


def send(source, target, sems, device):
    pltpu.make_async_remote_copy(
        src_ref=source, dst_ref=target, send_sem=sems[0], recv_sem=sems[1],
        device_id=device, device_id_type=pl.DeviceIdType.MESH,
    ).start()


def arrived(ref, sems, device):
    pltpu.make_async_remote_copy(
        src_ref=ref, dst_ref=ref, send_sem=sems[0], recv_sem=sems[1],
        device_id=device, device_id_type=pl.DeviceIdType.MESH,
    ).wait_recv()


def left(ref, sems, device):
    pltpu.make_async_remote_copy(
        src_ref=ref, dst_ref=ref, send_sem=sems[0], recv_sem=sems[1],
        device_id=device, device_id_type=pl.DeviceIdType.MESH,
    ).wait_send()


def shifted(place, step, count):
    return lax.rem(place + step, count)


class Reduce:
    def __init__(self, links, grads, pair, first, rest, second, sums, sems):
        self.k = links
        self.grads, self.pair, self.first, self.rest = grads, pair, first, rest
        self.second, self.sums, self.sems = second, sums, sems
        self.partner = links.device(core=1 - links.core)
        k = links
        self.major = [("z", k.nz), ("x", k.nx), ("y", k.ny)]
        self.minor = [
            (("y", k.ny), ("x", k.nx)), (("z", k.nz), ("y", k.ny)), (("z", k.nz), ("x", k.nx)),
        ]
        self.cell = 256 // (k.nx * k.ny)

    def at(self, name):
        return getattr(self.k, name)

    def sem(self, phase, color):
        return (self.sems.at[0, phase, color], self.sems.at[1, phase, color])

    def start_pair(self, color):
        away = pl.multiple_of(256 * (1 - self.k.core), 256)
        send(
            self.grads.at[color, :, pl.ds(away, 256)], self.pair.at[color],
            self.sem(0, color), self.partner,
        )

    def part(self, color, place):
        half = 256 * self.k.core
        if color == 0:
            return self.grads.at[color, place, pl.ds(pl.multiple_of(half, 256), 256)]
        rows = 256 // self.major[color][1]
        return self.grads.at[color, :, pl.ds(pl.multiple_of(half + place * rows, rows), rows)]

    def start_major(self, color):
        half = pl.ds(pl.multiple_of(256 * self.k.core, 256), 256)
        arrived(self.pair.at[color], self.sem(0, color), self.partner)
        for z in range(self.k.nz):
            self.grads[color, z, half] += self.pair[color, z]
        name, count = self.major[color]
        for step in range(1, count):
            place = shifted(self.at(name), step, count)
            send(
                self.part(color, place), self.first[color].at[step - 1],
                self.sem(1, color), self.k.device(**{name: place}),
            )

    def start_minor(self, color):
        name, count = self.major[color]
        place = self.at(name)
        if count > 1:
            arrived(self.first[color].at[0 : count - 1], self.sem(1, color), self.partner)
        half = 256 * self.k.core
        if color == 0:
            total = self.grads[0, place, pl.ds(pl.multiple_of(half, 256), 256)]
        else:
            rows = 256 // count
            total = self.grads[color, :, pl.ds(pl.multiple_of(half + place * rows, rows), rows)]
        for step in range(count - 1):
            total = total + self.first[color][step]
        (n0, c0), (n1, c1) = self.minor[color]
        self.rest[color][...] = total.reshape(c0, c1, self.cell, 128)
        for step0 in range(c0):
            for step1 in range(c1):
                if step0 == 0 and step1 == 0:
                    continue
                p0 = shifted(self.at(n0), step0, c0)
                p1 = shifted(self.at(n1), step1, c1)
                send(
                    self.rest[color].at[p0, p1], self.second[color].at[step0 * c1 + step1 - 1],
                    self.sem(2, color), self.k.device(**{n0: p0, n1: p1}),
                )

    def home(self, color):
        k = self.k
        inner = (k.x * k.ny + k.y) if color == 1 else (k.y * k.nx + k.x)
        return pl.ds(pl.multiple_of(256 * k.core + inner * self.cell, self.cell), self.cell)

    def start_spread(self, color):
        k = self.k
        (n0, c0), (n1, c1) = self.minor[color]
        if c0 * c1 > 1:
            arrived(self.second[color], self.sem(2, color), self.partner)
        total = self.rest[color][self.at(n0), self.at(n1)]
        for step in range(c0 * c1 - 1):
            total = total + self.second[color][step]
        self.sums[color, self.home(color)] = total
        for step0 in range(k.ny):
            for step1 in range(k.nx):
                if step0 == 0 and step1 == 0:
                    continue
                y = shifted(k.y, step0, k.ny)
                x = shifted(k.x, step1, k.nx)
                mine = self.sums.at[color, self.home(color)]
                send(mine, mine, self.sem(3, color), k.device(y=y, x=x))

    def start_share(self, color):
        k = self.k
        others = k.nx * k.ny - 1
        if others:
            arrived(self.sums.at[color, 0 : others * self.cell], self.sem(3, color), self.partner)
        half = pl.ds(pl.multiple_of(256 * k.core, 256), 256)
        mine = self.sums.at[color, half]
        send(mine, mine, self.sem(4, color), self.partner)

    def finish(self, color):
        k = self.k
        arrived(self.sums.at[color, 0:256], self.sem(4, color), self.partner)
        left(self.pair.at[color], self.sem(0, color), self.partner)
        count = self.major[color][1]
        if count > 1:
            left(self.first[color].at[0 : count - 1], self.sem(1, color), self.partner)
        if self.minor[color][0][1] * self.minor[color][1][1] > 1:
            left(self.second[color], self.sem(2, color), self.partner)
        others = k.nx * k.ny - 1
        if others:
            left(self.sums.at[color, 0 : others * self.cell], self.sem(3, color), self.partner)
        left(self.sums.at[color, 0:256], self.sem(4, color), self.partner)


def reduce_scratch(peers, nz):
    ny, nx = grid_of(peers)
    cell = 256 // (nx * ny)
    return [
        pltpu.VMEM((3, nz, 512, 128), F32),
        pltpu.VMEM((3, nz, 256, 128), F32),
        pltpu.VMEM((nz - 1, 256, 128), F32),
        pltpu.VMEM((max(nx - 1, 1), nz, 256 // nx, 128), F32),
        pltpu.VMEM((max(ny - 1, 1), nz, 256 // ny, 128), F32),
        pltpu.VMEM((ny, nx, cell, 128), F32),
        pltpu.VMEM((nz, ny, cell, 128), F32),
        pltpu.VMEM((nz, nx, cell, 128), F32),
        pltpu.VMEM((max(ny * nx - 1, 1), cell, 128), F32),
        pltpu.VMEM((nz * ny - 1, cell, 128), F32),
        pltpu.VMEM((nz * nx - 1, cell, 128), F32),
        pltpu.VMEM((3, 512, 128), F32),
        pltpu.SemaphoreType.DMA((2, 5, 3)),
    ]


def signal_all(links):
    barrier = pltpu.get_barrier_semaphore()
    k = links
    targets = []
    for step in range(1, k.nz):
        z = shifted(k.z, step, k.nz)
        for other in range(k.ny):
            targets.append(k.device(y=shifted(k.y, other, k.ny), z=z))
        for other in range(1, k.nx):
            targets.append(k.device(x=shifted(k.x, other, k.nx), z=z))
    for step in range(1, k.ny * k.nx * 2):
        targets.append((shifted(k.space, step, k.ny * k.nx * 2), k.z))
    for target in targets:
        pl.semaphore_signal(
            barrier, inc=1, device_id=target, device_id_type=pl.DeviceIdType.MESH
        )
    return barrier, len(targets)


def start_exchange(links, source, target, sems):
    peers = links.ny * links.nx * 2
    for step in range(1, peers):
        place = shifted(links.space, step, peers)
        send(source.at[place], target.at[links.space], sems, (place, links.z))
    target[links.space] = source[links.space]


def start_columns(links, source, target, sems):
    for step in range(1, links.nz):
        place = shifted(links.z, step, links.nz)
        send(source.at[place], target.at[links.z], sems, (links.space, place))
    target[links.z] = source[links.z]


def step_kernel(
    near, owner, features_hbm, mask_hbm, w_conv_hbm, w_down_hbm, cotangent_hbm,
    coarse_hbm, conv_sum, down_sum,
    features, mask, w_own, w_down, cotangent, w_conv,
    table, rims, windows, octants, factor, slopes, row_mask,
    cot_out, cot_in, piece_out, piece_in, dpiece_out, dpiece_in,
    halves, coarse_out, coarse_in, coarse, local_sems, front_sems,
    grads, pair, first_z, first_x, first_y, rest_0, rest_1, rest_2,
    second_0, second_1, second_2, sums, sems,
):
    links = Links()
    peers = links.ny * links.nx * 2
    nz = links.nz
    partner = links.device(core=1 - links.core)
    mine = links.z * 2
    reduce = Reduce(
        links, grads, pair, (first_z, first_x, first_y), (rest_0, rest_1, rest_2),
        (second_0, second_1, second_2), sums, sems,
    )

    def front(n):
        return (front_sems.at[0, n], front_sems.at[1, n])

    loads = [
        pltpu.make_async_copy(source, target, local_sems.at[n])
        for n, (source, target) in enumerate(
            (
                (w_conv_hbm, w_own), (cotangent_hbm, cotangent), (mask_hbm, mask),
                (features_hbm, features), (w_down_hbm, w_down),
            )
        )
    ]
    for load in loads:
        load.start()
    barrier, signals = signal_all(links)
    order = voxel_order()

    table[64] = jnp.zeros((64, 128), BF16)
    rims[0, 12:17] = jnp.zeros((5, 64, 128), BF16)
    rims[1, 8:12] = jnp.zeros((4, 64, 128), BF16)
    rims[1, 16] = jnp.zeros((64, 128), BF16)
    for z in range(nz):
        grads[1, z, 448:512] = jnp.zeros((64, 128), F32)
        grads[2, z, 416:512] = jnp.zeros((96, 128), F32)
    for r in range(2):
        halves[r, 8] = jnp.zeros((64, 128), BF16)
    loads[0].wait()
    for k in range(27):
        dx, d = k // 9, k % 9
        rows = pl.ds(pl.multiple_of(32 * links.z, 32), 32)
        w_conv[dx, rows, 128 * d : 128 * d + 128] = w_own[k]
    loads[1].wait()

    @pl.loop(0, peers)
    def _(d):
        cot_out[d, :, 0:64] = cotangent[2 * d]
        cot_out[d, :, 64:128] = cotangent[2 * d + 1]

    pl.semaphore_wait(barrier, signals)
    for step in range(1, nz):
        z = shifted(links.z, step, nz)
        rows = pl.ds(pl.multiple_of(32 * links.z + 16 * links.core, 16), 16)
        send(
            w_conv.at[:, rows], w_conv.at[:, rows],
            (front_sems.at[0, 5 + step], front_sems.at[1, 5 + step]), links.device(z=z),
        )
    start_exchange(links, cot_out, cot_in, front(0))

    loads[2].wait()
    loads[3].wait()

    @pl.loop(0, 8)
    def _(g):
        keep = mask[pl.ds(g, 1), :].astype(F32).astype(BF16)
        masked = features[g] * keep
        for h in range(2):
            turned = lax.dot_general(
                order, masked[:, 256 * h : 256 * h + 256], NT, preferred_element_type=F32
            )
            table[pl.ds(8 * g + 4 * h, 4)] = turned.astype(BF16).reshape(4, 64, 128)

    following = (shifted(links.space, 1, peers), links.z)
    previous = (shifted(links.space, peers - 1, peers), links.z)
    for j in range(8):
        rims[0, j] = table[8 * j + 7]
        rims[1, j] = table[8 * j]
    send(rims.at[0, 4:8], rims.at[0, 8:12], front(1), following)
    send(rims.at[1, 0:4], rims.at[1, 12:16], front(2), previous)
    for b in range(2):
        keep = mask[pl.ds(mine + b, 1), :].astype(F32)
        for h in range(2):
            wide = jnp.broadcast_to(keep[:, 256 * h : 256 * h + 256], (128, 256)).astype(BF16)
            turned = lax.dot_general(order, wide, NT, preferred_element_type=F32)
            row_mask[b, 256 * h : 256 * h + 256, :] = turned

        @pl.loop(1, 9)
        def _(xp):
            fill_plane(windows, table, near, b, mine, xp, 0)

    for step in range(1, nz):
        z = shifted(links.z, nz - step, nz)
        rows = pl.ds(pl.multiple_of(32 * z + 16 * links.core, 16), 16)
        piece = w_conv.at[:, rows]
        arrived(piece, (front_sems.at[0, 5 + step], front_sems.at[1, 5 + step]), partner)
        send(piece, piece, front(3), partner)
    arrived(rims.at[0, 8:12], front(1), previous)
    arrived(rims.at[1, 12:16], front(2), following)

    @pl.when(links.space == 0)
    def _():
        rims[0, 8:12] = jnp.zeros((4, 64, 128), BF16)

    @pl.when(links.space == peers - 1)
    def _():
        rims[1, 12:16] = jnp.zeros((4, 64, 128), BF16)

    for b in range(2):
        fill_plane(windows, rims.at[0], near, b, mine, 0, -1)
        fill_plane(windows, rims.at[1], near, b, mine, 9, 1)
    shared = w_conv.at[:, 0 : 16 * (nz - 1)]
    arrived(shared, front(3), partner)

    for b in range(2):
        total = None
        for dx in range(3):
            part = lax.dot_general(
                windows[b, dx : dx + 8].reshape(512, 1152), w_conv[dx], NT,
                preferred_element_type=F32,
            )
            total = part if total is None else total + part
        own = table[pl.ds(8 * (mine + b), 8)].astype(F32).reshape(512, 128)
        pre = own + total
        keep = row_mask[b]
        gate = jax.nn.sigmoid(pre)
        hidden = (keep * (pre * gate)).astype(BF16).reshape(4, 2, 4, 16, 128)
        factor[b] = keep * gate * (1.0 + pre * (1.0 - gate))
        for a in range(2):
            for t in range(4):
                octants[4 * a + t, 64 * b : 64 * b + 64, :] = hidden[:, a, t].reshape(64, 128)
    loads[4].wait()
    total = None
    for o in range(8):
        part = lax.dot_general(w_down[o], octants[o], NT, preferred_element_type=F32)
        total = part if total is None else total + part
    piece_out[...] = total.astype(BF16).reshape(nz, 64, 128)
    start_columns(links, piece_out, piece_in, front(4))

    arrived(cot_in.at[0 : peers - 1], front(0), partner)
    owners = [owner[g, 0] for g in range(8)]
    low = lax.broadcasted_iota(jnp.int32, (64, 128), 1) < 64
    for z in range(4):
        parts = []
        for i in range(2):
            g = 2 * z + i
            rank = jnp.int32(0)
            for h in range(g):
                rank = rank + jnp.where(owners[h] == owners[g], 1, 0)
            value = cot_in[owners[g]].astype(F32)
            parts.append(jnp.where(rank == i, value, pltpu.roll(value, 64, 1)))
        dpiece_out[z] = jnp.where(low, parts[0], parts[1]).astype(BF16)
    start_columns(links, dpiece_out, dpiece_in, front(5))

    arrived(piece_in.at[0 : nz - 1], front(4), partner)
    for g in range(8):
        value = piece_in[g // 2].astype(F32)
        swapped = pltpu.roll(value, 64, 1)
        first, other = (value, swapped) if g % 2 == 0 else (swapped, value)
        halves[0, g] = jnp.where(low, first, 0.0).astype(BF16)
        halves[1, g] = jnp.where(low, 0.0, other).astype(BF16)

    @pl.loop(0, peers)
    def _(d):
        place_0 = jnp.int32(8)
        place_1 = jnp.int32(8)
        for g in range(7, -1, -1):
            hit = owners[g] == d
            place_1 = jnp.where(hit, place_0, place_1)
            place_0 = jnp.where(hit, g, place_0)
        coarse_out[d] = halves[0, place_0] + halves[1, place_1]

    start_exchange(links, coarse_out, coarse_in, front(9))

    arrived(dpiece_in.at[0 : nz - 1], front(5), partner)
    piece = dpiece_in[...].reshape(256, 128)
    piece_rows = piece.astype(F32).T.astype(BF16)
    for o in range(8):
        part = jnp.dot(piece, octants[o], preferred_element_type=F32)
        for z in range(4):
            grads[0, z, 64 * o : 64 * o + 64, :] = part[64 * z : 64 * z + 64]
    reduce.start_pair(0)
    for b in range(2):
        for a in range(2):
            for t in range(4):
                o = 4 * a + t
                dhidden = jnp.dot(
                    piece_rows[64 * b : 64 * b + 64], w_down[o], preferred_element_type=F32
                ).reshape(4, 16, 128)
                for qx in range(4):
                    row = 64 * (2 * qx + a) + 16 * t
                    slopes[b, row : row + 16, :] = dhidden[qx] * factor[b, row : row + 16, :]
    turned = [slopes[b].astype(BF16).astype(F32).T.astype(BF16) for b in range(2)]
    for dx in range(3):
        total = None
        for b in range(2):
            part = jnp.dot(
                turned[b], windows[b, dx : dx + 8].reshape(512, 1152), preferred_element_type=F32
            )
            total = part if total is None else total + part
        for d in range(9):
            k = 9 * dx + d
            color, row = (1, 32 * k) if k < 14 else (2, 32 * (k - 14))
            for z in range(4):
                grads[color, z, row : row + 32, :] = total[
                    32 * z : 32 * z + 32, 128 * d : 128 * d + 128
                ]
        if dx == 0:
            reduce.start_major(0)
        else:
            reduce.start_pair(dx)
    reduce.start_major(1)
    reduce.start_major(2)
    for color in range(3):
        reduce.start_minor(color)
    for color in range(3):
        reduce.start_spread(color)

    arrived(coarse_in.at[0 : peers - 1], front(9), partner)

    @pl.loop(0, peers)
    def _(d):
        coarse[2 * d] = coarse_in[d, :, 0:64]
        coarse[2 * d + 1] = coarse_in[d, :, 64:128]

    store = pltpu.make_async_copy(coarse, coarse_hbm, local_sems.at[5])
    store.start()
    for color in range(3):
        reduce.start_share(color)
    for color in range(3):
        reduce.finish(color)
    for o in range(8):
        down_sum[o] = sums[0, 64 * o : 64 * o + 64]
    for k in range(27):
        color, row = (1, 32 * k) if k < 14 else (2, 32 * (k - 14))
        conv_sum[k] = sums[color, row : row + 32]
    left(cot_out.at[0 : peers - 1], front(0), partner)
    left(rims.at[0, 4:8], front(1), partner)
    left(rims.at[1, 0:4], front(2), partner)
    left(shared, front(3), partner)
    left(piece_out.at[0 : nz - 1], front(4), partner)
    left(dpiece_out.at[0 : nz - 1], front(5), partner)
    for step in range(1, nz):
        left(
            w_conv.at[:, 0:16],
            (front_sems.at[0, 5 + step], front_sems.at[1, 5 + step]), partner,
        )
    left(coarse_out.at[0 : peers - 1], front(9), partner)
    store.wait()


def local(features, voxel_mask, neighbors, w_conv, w_down, coarse_owner, cotangent):
    peers = lax.axis_size("space")
    nz = lax.axis_size("chan")
    vmem = pl.BlockSpec(memory_space=pltpu.VMEM)
    smem = pl.BlockSpec(memory_space=pltpu.SMEM)
    anywhere = pl.BlockSpec(memory_space=pl.ANY)
    return pl.pallas_call(
        step_kernel,
        out_shape=(
            jax.ShapeDtypeStruct(cotangent.shape, BF16),
            jax.ShapeDtypeStruct((27, 32, 128), F32),
            jax.ShapeDtypeStruct((8, 64, 128), F32),
        ),
        in_specs=[smem, smem] + [anywhere] * 5,
        out_specs=(anywhere, vmem, vmem),
        scratch_shapes=[
            pltpu.VMEM((8, 128, 512), BF16),
            pltpu.VMEM((8, 512), jnp.int32),
            pltpu.VMEM((27, 32, 128), BF16),
            pltpu.VMEM((8, 256, 128), BF16),
            pltpu.VMEM(cotangent.shape, BF16),
            pltpu.VMEM((3, 128, 1152), BF16),
            pltpu.VMEM((65, 64, 128), BF16),
            pltpu.VMEM((2, 17, 64, 128), BF16),
            pltpu.VMEM((2, 10, 64, 1152), BF16),
            pltpu.VMEM((8, 128, 128), BF16),
            pltpu.VMEM((2, 512, 128), F32),
            pltpu.VMEM((2, 512, 128), F32),
            pltpu.VMEM((2, 512, 128), F32),
            pltpu.VMEM((peers, 64, 128), BF16),
            pltpu.VMEM((peers, 64, 128), BF16),
            pltpu.VMEM((nz, 64, 128), BF16),
            pltpu.VMEM((nz, 64, 128), BF16),
            pltpu.VMEM((nz, 64, 128), BF16),
            pltpu.VMEM((nz, 64, 128), BF16),
            pltpu.VMEM((2, 9, 64, 128), BF16),
            pltpu.VMEM((peers, 64, 128), BF16),
            pltpu.VMEM((peers, 64, 128), BF16),
            pltpu.VMEM(cotangent.shape, BF16),
            pltpu.SemaphoreType.DMA((6,)),
            pltpu.SemaphoreType.DMA((2, 10)),
        ]
        + reduce_scratch(peers, nz),
        compiler_params=pltpu.CompilerParams(
            vmem_limit_bytes=56 << 20, collective_id=0, has_side_effects=True
        ),
    )(neighbors, coarse_owner, features, voxel_mask, w_conv, w_down, cotangent)


def solution(mesh):
    in_specs = (
        P("space", None, None),
        P("space", None),
        P("space", None),
        P(None, "chan", None),
        P(),
        P("space", None),
        P("space", "chan", None),
    )
    out_specs = (P("space", "chan", None), P(None, "chan", None), P(None, "chan", None))
    return jax.shard_map(local, mesh=mesh, in_specs=in_specs, out_specs=out_specs, check_vma=False)
```

```python
import jax
import jax.numpy as jnp
from jax import lax
from jax.experimental import pallas as pl
from jax.experimental.pallas import tpu as pltpu
from jax.sharding import PartitionSpec as P

F32 = jnp.float32
BF16 = jnp.bfloat16
NT = (((1,), (1,)), ((), ()))


def voxel_order():
    row = lax.broadcasted_iota(jnp.int32, (256, 256), 0)
    col = lax.broadcasted_iota(jnp.int32, (256, 256), 1)
    y = ((row >> 2) & 3) * 2 + ((row >> 5) & 1)
    z = (row & 3) * 2 + ((row >> 4) & 1)
    source = (row & ~63) + y * 8 + z
    return (source == col).astype(F32).astype(BF16)


def fill_plane(windows, planes, near, b, mine, xp, sx):
    qy = (lax.broadcasted_iota(jnp.int32, (16, 128), 0) >> 2) & 3
    qz = lax.broadcasted_iota(jnp.int32, (16, 128), 0) & 3
    loaded = {}
    for sy in (-1, 0, 1):
        for sz in (-1, 0, 1):
            position = 9 * (sx + 1) + 3 * (sy + 1) + (sz + 1)
            if position == 13:
                slot = mine + b
            else:
                slot = near[mine + b, position if position < 13 else position - 1]
            if sx == 0:
                plane = jnp.where((slot < 0) | (slot > 7), 64, 8 * slot + xp - 1)
            else:
                plane = jnp.where(slot < 0, 16, slot)
            loaded[sy, sz] = planes[plane].astype(F32).reshape(4, 16, 128)

    def merged(oy, sz, tile):
        inner = loaded[0, sz][tile]
        if oy == 0:
            return inner
        return jnp.where(qy == (3 if oy < 0 else 0), loaded[oy, sz][tile], inner)

    def turned(value, shift):
        return value if shift % 16 == 0 else pltpu.roll(value, shift % 16, 0)

    for i in range(4):
        for j in range(4):
            oy = (-1, 0, 0, 1)[i]
            oz = (-1, 0, 0, 1)[j]
            tile = (1, 0, 1, 0)[i] * 2 + (1, 0, 1, 0)[j]
            value = turned(merged(oy, 0, tile), -4 * oy - oz)
            if oz != 0:
                edge = turned(merged(oy, oz, tile), -4 * oy + 3 * oz)
                value = jnp.where(qz == (0 if oz < 0 else 3), edge, value)
            value = value.astype(BF16)
            for p in range(2):
                for e in range(2):
                    dy, dz = i - p, j - e
                    if 0 <= dy <= 2 and 0 <= dz <= 2:
                        row = 32 * p + 16 * e
                        col = 128 * (3 * dy + dz)
                        windows[b, xp, row : row + 16, col : col + 128] = value


def grid_of(peers):
    chips = peers // 2
    across = 4 if chips == 16 else (2 if chips == 4 else 1)
    return chips // across, across


class Links:
    def __init__(self):
        self.ny, self.nx = grid_of(lax.axis_size("space"))
        self.nz = lax.axis_size("chan")
        space = lax.axis_index("space")
        self.space = space
        self.z = lax.axis_index("chan")
        self.core = lax.rem(space, 2)
        self.x = lax.rem(space // 2, self.nx)
        self.y = space // (2 * self.nx)

    def device(self, y=None, x=None, z=None, core=None):
        y = self.y if y is None else y
        x = self.x if x is None else x
        z = self.z if z is None else z
        core = self.core if core is None else core
        return ((y * self.nx + x) * 2 + core, z)


def send(source, target, sems, device):
    pltpu.make_async_remote_copy(
        src_ref=source, dst_ref=target, send_sem=sems[0], recv_sem=sems[1],
        device_id=device, device_id_type=pl.DeviceIdType.MESH,
    ).start()


def arrived(ref, sems, device):
    pltpu.make_async_remote_copy(
        src_ref=ref, dst_ref=ref, send_sem=sems[0], recv_sem=sems[1],
        device_id=device, device_id_type=pl.DeviceIdType.MESH,
    ).wait_recv()


def left(ref, sems, device):
    pltpu.make_async_remote_copy(
        src_ref=ref, dst_ref=ref, send_sem=sems[0], recv_sem=sems[1],
        device_id=device, device_id_type=pl.DeviceIdType.MESH,
    ).wait_send()


def shifted(place, step, count):
    return lax.rem(place + step, count)


HALF = (256, 128, 128, 256)
FULL = (256, 128, 128, 192)
LEAD = ("z", "x", "y", "z")
CONV_ROWS = [(3, 32 * k + (64 if k > 5 else 0)) for k in range(11)]
CONV_ROWS += [(1, 32 * k) for k in range(8)] + [(2, 32 * k) for k in range(8)]


def group_of(color, ny, nx, nz):
    return {
        "z": (("y", ny), ("x", nx)), "x": (("z", nz), ("y", ny)), "y": (("z", nz), ("x", nx)),
    }[LEAD[color]]


class Reduce:
    def __init__(self, links, grads, pair, first, rest, second, sums, sems):
        self.k = links
        self.grads, self.pair, self.first, self.rest = grads, pair, first, rest
        self.second, self.sums, self.sems = second, sums, sems
        self.partner = links.device(core=1 - links.core)
        k = links
        self.counts = {"z": k.nz, "x": k.nx, "y": k.ny}
        self.minor = [group_of(color, k.ny, k.nx, k.nz) for color in range(4)]
        self.cell = [half // (k.nx * k.ny) for half in HALF]

    def at(self, name):
        return getattr(self.k, name)

    def sem(self, phase, color):
        return (self.sems.at[0, phase, color], self.sems.at[1, phase, color])

    def start_pair(self, color):
        away = pl.multiple_of(HALF[color] * (1 - self.k.core), 128)
        send(
            self.grads.at[color, :, pl.ds(away, FULL[color])],
            self.pair.at[color, :, 0 : FULL[color]], self.sem(0, color), self.partner,
        )

    def part(self, color, place):
        base = HALF[color] * self.k.core
        if LEAD[color] == "z":
            return place, pl.ds(pl.multiple_of(base, 128), FULL[color])
        rows = HALF[color] // self.counts[LEAD[color]]
        return slice(None), pl.ds(pl.multiple_of(base + place * rows, rows), rows)

    def start_major(self, color):
        full = FULL[color]
        rows = pl.ds(pl.multiple_of(HALF[color] * self.k.core, 128), full)
        arrived(self.pair.at[color, :, 0:full], self.sem(0, color), self.partner)
        for z in range(self.k.nz):
            self.grads[color, z, rows] += self.pair[color, z, 0:full]
        name = LEAD[color]
        count = self.counts[name]
        for step in range(1, count):
            place = shifted(self.at(name), step, count)
            chunk, span = self.part(color, place)
            send(
                self.grads.at[color, chunk, span], self.first[color].at[step - 1],
                self.sem(1, color), self.k.device(**{name: place}),
            )

    def start_minor(self, color):
        name = LEAD[color]
        count = self.counts[name]
        if count > 1:
            arrived(self.first[color].at[0 : count - 1], self.sem(1, color), self.partner)
        chunk, span = self.part(color, self.at(name))
        total = self.grads[color, chunk, span]
        for step in range(count - 1):
            total = total + self.first[color][step]
        cell = self.cell[color]
        used = FULL[color] // cell
        if LEAD[color] != "z":
            used = self.rest[color].shape[0]
        self.rest[color][0:used] = total.reshape(used, cell, 128)
        (n0, c0), (n1, c1) = self.minor[color]
        for step0 in range(c0):
            for step1 in range(c1):
                if step0 == 0 and step1 == 0:
                    continue
                p0 = shifted(self.at(n0), step0, c0)
                p1 = shifted(self.at(n1), step1, c1)
                send(
                    self.rest[color].at[p0 * c1 + p1],
                    self.second[color].at[step0 * c1 + step1 - 1],
                    self.sem(2, color), self.k.device(**{n0: p0, n1: p1}),
                )

    def home(self, color):
        k = self.k
        inner = (k.x * k.ny + k.y) if LEAD[color] == "x" else (k.y * k.nx + k.x)
        cell = self.cell[color]
        return pl.ds(pl.multiple_of(HALF[color] * k.core + inner * cell, cell), cell)

    def start_spread(self, color):
        k = self.k
        (n0, c0), (n1, c1) = self.minor[color]
        if c0 * c1 > 1:
            arrived(self.second[color], self.sem(2, color), self.partner)
        total = self.rest[color][self.at(n0) * c1 + self.at(n1)]
        for step in range(c0 * c1 - 1):
            total = total + self.second[color][step]
        self.sums[color, self.home(color)] = total
        for step0 in range(k.ny):
            for step1 in range(k.nx):
                if step0 == 0 and step1 == 0:
                    continue
                y = shifted(k.y, step0, k.ny)
                x = shifted(k.x, step1, k.nx)
                mine = self.sums.at[color, self.home(color)]
                send(mine, mine, self.sem(3, color), k.device(y=y, x=x))

    def others(self, color):
        return self.sums.at[color, 0 : (self.k.nx * self.k.ny - 1) * self.cell[color]]

    def start_share(self, color):
        if self.k.nx * self.k.ny > 1:
            arrived(self.others(color), self.sem(3, color), self.partner)
        half = HALF[color]
        mine = self.sums.at[color, pl.ds(pl.multiple_of(half * self.k.core, 128), half)]
        send(mine, mine, self.sem(4, color), self.partner)

    def finish(self, color):
        half = self.sums.at[color, 0 : HALF[color]]
        arrived(half, self.sem(4, color), self.partner)
        left(self.pair.at[color, :, 0 : FULL[color]], self.sem(0, color), self.partner)
        count = self.counts[LEAD[color]]
        if count > 1:
            left(self.first[color].at[0 : count - 1], self.sem(1, color), self.partner)
        if self.minor[color][0][1] * self.minor[color][1][1] > 1:
            left(self.second[color], self.sem(2, color), self.partner)
        if self.k.nx * self.k.ny > 1:
            left(self.others(color), self.sem(3, color), self.partner)
        left(half, self.sem(4, color), self.partner)


def reduce_scratch(peers, nz):
    ny, nx = grid_of(peers)
    counts = {"z": nz, "x": nx, "y": ny}
    first, rest, second = [], [], []
    for color in range(4):
        count = counts[LEAD[color]]
        if LEAD[color] == "z":
            shape = (max(count - 1, 1), FULL[color], 128)
        else:
            shape = (max(count - 1, 1), nz, HALF[color] // count, 128)
        first.append(pltpu.VMEM(shape, F32))
        (_, c0), (_, c1) = group_of(color, ny, nx, nz)
        cell = HALF[color] // (nx * ny)
        rest.append(pltpu.VMEM((c0 * c1, cell, 128), F32))
        second.append(pltpu.VMEM((max(c0 * c1 - 1, 1), cell, 128), F32))
    return [
        pltpu.VMEM((4, nz, 512, 128), F32), pltpu.VMEM((4, nz, 256, 128), F32),
        *first, *rest, *second,
        pltpu.VMEM((4, 512, 128), F32), pltpu.SemaphoreType.DMA((2, 5, 4)),
    ]


def signal_all(links):
    barrier = pltpu.get_barrier_semaphore()
    k = links
    targets = []
    for step in range(1, k.nz):
        z = shifted(k.z, step, k.nz)
        for other in range(k.ny):
            targets.append(k.device(y=shifted(k.y, other, k.ny), z=z))
        for other in range(1, k.nx):
            targets.append(k.device(x=shifted(k.x, other, k.nx), z=z))
    for step in range(1, k.ny * k.nx * 2):
        targets.append((shifted(k.space, step, k.ny * k.nx * 2), k.z))
    for target in targets:
        pl.semaphore_signal(
            barrier, inc=1, device_id=target, device_id_type=pl.DeviceIdType.MESH
        )
    return barrier, len(targets)


def start_exchange(links, source, target, sems):
    peers = links.ny * links.nx * 2
    for step in range(1, peers):
        place = shifted(links.space, step, peers)
        send(source.at[place], target.at[links.space], sems, (place, links.z))
    target[links.space] = source[links.space]


def start_columns(links, source, target, sems):
    for step in range(1, links.nz):
        place = shifted(links.z, step, links.nz)
        send(source.at[place], target.at[links.z], sems, (links.space, place))
    target[links.z] = source[links.z]


def step_kernel(
    near, owner, features_hbm, mask_hbm, w_conv_hbm, w_down_hbm, cotangent_hbm,
    coarse_hbm, conv_hbm, down_hbm,
    features, mask, w_own, w_down, cotangent, w_conv,
    table, rims, windows, octants, factor, slopes, row_mask,
    cot_out, cot_in, piece_out, piece_in, dpiece_out, dpiece_in,
    halves, coarse_out, coarse_in, local_sems, front_sems,
    grads, pair, first_0, first_1, first_2, first_3, rest_0, rest_1, rest_2, rest_3,
    second_0, second_1, second_2, second_3, sums, sems,
):
    links = Links()
    peers = links.ny * links.nx * 2
    nz = links.nz
    partner = links.device(core=1 - links.core)
    mine = links.z * 2
    reduce = Reduce(
        links, grads, pair, (first_0, first_1, first_2, first_3),
        (rest_0, rest_1, rest_2, rest_3), (second_0, second_1, second_2, second_3), sums, sems,
    )

    def front(n):
        return (front_sems.at[0, n], front_sems.at[1, n])

    loads = [
        pltpu.make_async_copy(source, target, local_sems.at[n])
        for n, (source, target) in enumerate(
            (
                (w_conv_hbm, w_own), (cotangent_hbm, cotangent), (mask_hbm, mask),
                (features_hbm, features), (w_down_hbm, w_down),
            )
        )
    ]
    for load in loads:
        load.start()
    barrier, signals = signal_all(links)
    order = voxel_order()

    table[64] = jnp.zeros((64, 128), BF16)
    rims[0, 12:17] = jnp.zeros((5, 64, 128), BF16)
    rims[1, 8:12] = jnp.zeros((4, 64, 128), BF16)
    rims[1, 16] = jnp.zeros((64, 128), BF16)
    for z in range(nz):
        grads[3, z, 416:448] = jnp.zeros((32, 128), F32)
    rest_3[...] = jnp.zeros_like(rest_3)
    for r in range(2):
        halves[r, 8] = jnp.zeros((64, 128), BF16)
    loads[0].wait()
    for k in range(27):
        dx, d = k // 9, k % 9
        rows = pl.ds(pl.multiple_of(32 * links.z, 32), 32)
        w_conv[dx, rows, 128 * d : 128 * d + 128] = w_own[k]
    loads[1].wait()

    @pl.loop(0, peers)
    def _(d):
        cot_out[d, :, 0:64] = cotangent[2 * d]
        cot_out[d, :, 64:128] = cotangent[2 * d + 1]

    pl.semaphore_wait(barrier, signals)
    for step in range(1, nz):
        z = shifted(links.z, step, nz)
        rows = pl.ds(pl.multiple_of(32 * links.z + 16 * links.core, 16), 16)
        send(
            w_conv.at[:, rows], w_conv.at[:, rows],
            (front_sems.at[0, 5 + step], front_sems.at[1, 5 + step]), links.device(z=z),
        )
    start_exchange(links, cot_out, cot_in, front(0))

    loads[2].wait()
    loads[3].wait()

    @pl.loop(0, 8)
    def _(g):
        keep = mask[pl.ds(g, 1), :].astype(F32).astype(BF16)
        masked = features[g] * keep
        for h in range(2):
            turned = lax.dot_general(
                order, masked[:, 256 * h : 256 * h + 256], NT, preferred_element_type=F32
            )
            table[pl.ds(8 * g + 4 * h, 4)] = turned.astype(BF16).reshape(4, 64, 128)

    following = (shifted(links.space, 1, peers), links.z)
    previous = (shifted(links.space, peers - 1, peers), links.z)
    for j in range(8):
        rims[0, j] = table[8 * j + 7]
        rims[1, j] = table[8 * j]
    send(rims.at[0, 4:8], rims.at[0, 8:12], front(1), following)
    send(rims.at[1, 0:4], rims.at[1, 12:16], front(2), previous)
    for b in range(2):
        keep = mask[pl.ds(mine + b, 1), :].astype(F32)
        for h in range(2):
            wide = jnp.broadcast_to(keep[:, 256 * h : 256 * h + 256], (128, 256)).astype(BF16)
            turned = lax.dot_general(order, wide, NT, preferred_element_type=F32)
            row_mask[b, 256 * h : 256 * h + 256, :] = turned

        @pl.loop(1, 9)
        def _(xp):
            fill_plane(windows, table, near, b, mine, xp, 0)

    for step in range(1, nz):
        z = shifted(links.z, nz - step, nz)
        rows = pl.ds(pl.multiple_of(32 * z + 16 * links.core, 16), 16)
        piece = w_conv.at[:, rows]
        arrived(piece, (front_sems.at[0, 5 + step], front_sems.at[1, 5 + step]), partner)
        send(piece, piece, front(3), partner)
    arrived(rims.at[0, 8:12], front(1), previous)
    arrived(rims.at[1, 12:16], front(2), following)

    @pl.when(links.space == 0)
    def _():
        rims[0, 8:12] = jnp.zeros((4, 64, 128), BF16)

    @pl.when(links.space == peers - 1)
    def _():
        rims[1, 12:16] = jnp.zeros((4, 64, 128), BF16)

    for b in range(2):
        fill_plane(windows, rims.at[0], near, b, mine, 0, -1)
        fill_plane(windows, rims.at[1], near, b, mine, 9, 1)
    arrived(cot_in.at[0 : peers - 1], front(0), partner)
    owners = [owner[0, g] for g in range(8)]
    low = lax.broadcasted_iota(jnp.int32, (64, 128), 1) < 64
    for z in range(4):
        parts = []
        for i in range(2):
            g = 2 * z + i
            rank = jnp.int32(0)
            for h in range(g):
                rank = rank + jnp.where(owners[h] == owners[g], 1, 0)
            value = cot_in[owners[g]].astype(F32)
            parts.append(jnp.where(rank == i, value, pltpu.roll(value, 64, 1)))
        dpiece_out[z] = jnp.where(low, parts[0], parts[1]).astype(BF16)
    start_columns(links, dpiece_out, dpiece_in, front(5))

    shared = w_conv.at[:, 0 : 16 * (nz - 1)]
    arrived(shared, front(3), partner)

    for b in range(2):
        total = None
        for dx in range(3):
            part = lax.dot_general(
                windows[b, dx : dx + 8].reshape(512, 1152), w_conv[dx], NT,
                preferred_element_type=F32,
            )
            total = part if total is None else total + part
        own = table[pl.ds(8 * (mine + b), 8)].astype(F32).reshape(512, 128)
        pre = own + total
        keep = row_mask[b]
        gate = jax.nn.sigmoid(pre)
        hidden = (keep * (pre * gate)).astype(BF16).reshape(4, 2, 4, 16, 128)
        factor[b] = keep * gate * (1.0 + pre * (1.0 - gate))
        for a in range(2):
            for t in range(4):
                octants[4 * a + t, 64 * b : 64 * b + 64, :] = hidden[:, a, t].reshape(64, 128)
    loads[4].wait()
    total = None
    for o in range(8):
        part = lax.dot_general(w_down[o], octants[o], NT, preferred_element_type=F32)
        total = part if total is None else total + part
    piece_out[...] = total.astype(BF16).reshape(nz, 64, 128)
    start_columns(links, piece_out, piece_in, front(4))

    arrived(dpiece_in.at[0 : nz - 1], front(5), partner)
    piece = dpiece_in[...].reshape(256, 128)
    piece_rows = piece.astype(F32).T.astype(BF16)
    for o in range(8):
        part = jnp.dot(piece, octants[o], preferred_element_type=F32)
        for z in range(4):
            grads[0, z, 64 * o : 64 * o + 64, :] = part[64 * z : 64 * z + 64]
    reduce.start_pair(0)
    for b in range(2):
        for a in range(2):
            for t in range(4):
                o = 4 * a + t
                dhidden = jnp.dot(
                    piece_rows[64 * b : 64 * b + 64], w_down[o], preferred_element_type=F32
                ).reshape(4, 16, 128)
                for qx in range(4):
                    row = 64 * (2 * qx + a) + 16 * t
                    slopes[b, row : row + 16, :] = dhidden[qx] * factor[b, row : row + 16, :]
    arrived(piece_in.at[0 : nz - 1], front(4), partner)
    for g in range(8):
        value = piece_in[g // 2].astype(F32)
        swapped = pltpu.roll(value, 64, 1)
        first, other = (value, swapped) if g % 2 == 0 else (swapped, value)
        halves[0, g] = jnp.where(low, first, 0.0).astype(BF16)
        halves[1, g] = jnp.where(low, 0.0, other).astype(BF16)

    @pl.loop(0, peers)
    def _(d):
        place_0 = jnp.int32(8)
        place_1 = jnp.int32(8)
        for g in range(7, -1, -1):
            hit = owners[g] == d
            place_1 = jnp.where(hit, place_0, place_1)
            place_0 = jnp.where(hit, g, place_0)
        coarse_out[d] = halves[0, place_0] + halves[1, place_1]

    start_exchange(links, coarse_out, coarse_in, front(9))

    turned = [slopes[b].astype(BF16).astype(F32).T.astype(BF16) for b in range(2)]
    for dx in range(3):
        total = None
        for b in range(2):
            part = jnp.dot(
                turned[b], windows[b, dx : dx + 8].reshape(512, 1152), preferred_element_type=F32
            )
            total = part if total is None else total + part
        for d in range(9):
            k = 9 * dx + d
            color, row = CONV_ROWS[k]
            for z in range(4):
                grads[color, z, row : row + 32, :] = total[
                    32 * z : 32 * z + 32, 128 * d : 128 * d + 128
                ]
        if dx == 0:
            reduce.start_major(0)
        elif dx == 1:
            reduce.start_pair(3)
    reduce.start_pair(1)
    reduce.start_pair(2)
    reduce.start_major(3)
    reduce.start_major(1)
    reduce.start_major(2)
    for color in (0, 1, 2, 3):
        reduce.start_minor(color)
    for color in (0, 1, 2, 3):
        reduce.start_spread(color)

    arrived(coarse_in.at[0 : peers - 1], front(9), partner)

    stores = [pltpu.make_async_copy(coarse_in, coarse_hbm, local_sems.at[5])]
    stores[0].start()
    for color in (0, 1, 2, 3):
        reduce.start_share(color)
    for color in range(4):
        reduce.finish(color)
        if color == 0:
            for o in range(8):
                pltpu.make_async_copy(
                    sums.at[0, 64 * o : 64 * o + 64], down_hbm.at[o], local_sems.at[6]
                ).start()
        for k in range(27):
            if CONV_ROWS[k][0] == color:
                row = CONV_ROWS[k][1]
                pltpu.make_async_copy(
                    sums.at[color, row : row + 32], conv_hbm.at[k], local_sems.at[7]
                ).start()
    stores.append(pltpu.make_async_copy(down_hbm, down_hbm, local_sems.at[6]))
    stores.append(pltpu.make_async_copy(conv_hbm, conv_hbm, local_sems.at[7]))
    left(cot_out.at[0 : peers - 1], front(0), partner)
    left(rims.at[0, 4:8], front(1), partner)
    left(rims.at[1, 0:4], front(2), partner)
    left(shared, front(3), partner)
    left(piece_out.at[0 : nz - 1], front(4), partner)
    left(dpiece_out.at[0 : nz - 1], front(5), partner)
    for step in range(1, nz):
        left(
            w_conv.at[:, 0:16],
            (front_sems.at[0, 5 + step], front_sems.at[1, 5 + step]), partner,
        )
    left(coarse_out.at[0 : peers - 1], front(9), partner)
    for copy in stores:
        copy.wait()


def local(features, voxel_mask, neighbors, w_conv, w_down, coarse_owner, cotangent):
    peers = lax.axis_size("space")
    nz = lax.axis_size("chan")
    smem = pl.BlockSpec(memory_space=pltpu.SMEM)
    anywhere = pl.BlockSpec(memory_space=pl.ANY)
    coarse_pairs, conv_sum, down_sum = pl.pallas_call(
        step_kernel,
        out_shape=(
            jax.ShapeDtypeStruct((peers, 64, 128), BF16),
            jax.ShapeDtypeStruct((27, 32, 128), F32),
            jax.ShapeDtypeStruct((8, 64, 128), F32),
        ),
        in_specs=[smem, smem] + [anywhere] * 5,
        out_specs=(anywhere, anywhere, anywhere),
        scratch_shapes=[
            pltpu.VMEM((8, 128, 512), BF16),
            pltpu.VMEM((8, 512), jnp.int32),
            pltpu.VMEM((27, 32, 128), BF16),
            pltpu.VMEM((8, 256, 128), BF16),
            pltpu.VMEM(cotangent.shape, BF16),
            pltpu.VMEM((3, 128, 1152), BF16),
            pltpu.VMEM((65, 64, 128), BF16),
            pltpu.VMEM((2, 17, 64, 128), BF16),
            pltpu.VMEM((2, 10, 64, 1152), BF16),
            pltpu.VMEM((8, 128, 128), BF16),
            pltpu.VMEM((2, 512, 128), F32),
            pltpu.VMEM((2, 512, 128), F32),
            pltpu.VMEM((2, 512, 128), F32),
            pltpu.VMEM((peers, 64, 128), BF16),
            pltpu.VMEM((peers, 64, 128), BF16),
            pltpu.VMEM((nz, 64, 128), BF16),
            pltpu.VMEM((nz, 64, 128), BF16),
            pltpu.VMEM((nz, 64, 128), BF16),
            pltpu.VMEM((nz, 64, 128), BF16),
            pltpu.VMEM((2, 9, 64, 128), BF16),
            pltpu.VMEM((peers, 64, 128), BF16),
            pltpu.VMEM((peers, 64, 128), BF16),
            pltpu.SemaphoreType.DMA((8,)),
            pltpu.SemaphoreType.DMA((2, 10)),
        ]
        + reduce_scratch(peers, nz),
        compiler_params=pltpu.CompilerParams(
            vmem_limit_bytes=56 << 20, collective_id=0, has_side_effects=True
        ),
    )(neighbors, coarse_owner.reshape(1, 8), features, voxel_mask, w_conv, w_down, cotangent)
    pairs = coarse_pairs.reshape(peers, 64, 2, 64).transpose(0, 2, 1, 3)
    return (pairs.reshape(cotangent.shape), conv_sum, down_sum)


def solution(mesh):
    in_specs = (
        P("space", None, None),
        P("space", None),
        P("space", None),
        P(None, "chan", None),
        P(),
        P("space", None),
        P("space", "chan", None),
    )
    out_specs = (P("space", "chan", None), P(None, "chan", None), P(None, "chan", None))
    return jax.shard_map(local, mesh=mesh, in_specs=in_specs, out_specs=out_specs, check_vma=False)
```

```python
import jax
import jax.numpy as jnp
from jax import lax
from jax.experimental import pallas as pl
from jax.experimental.pallas import tpu as pltpu
from jax.sharding import PartitionSpec as P

F32 = jnp.float32
BF16 = jnp.bfloat16
NT = (((1,), (1,)), ((), ()))


def voxel_order():
    row = lax.broadcasted_iota(jnp.int32, (256, 256), 0)
    col = lax.broadcasted_iota(jnp.int32, (256, 256), 1)
    y = ((row >> 2) & 3) * 2 + ((row >> 5) & 1)
    z = (row & 3) * 2 + ((row >> 4) & 1)
    source = (row & ~63) + y * 8 + z
    return (source == col).astype(F32).astype(BF16)


def fill_plane(windows, planes, near, b, mine, xp, sx):
    qy = (lax.broadcasted_iota(jnp.int32, (16, 128), 0) >> 2) & 3
    qz = lax.broadcasted_iota(jnp.int32, (16, 128), 0) & 3
    loaded = {}
    for sy in (-1, 0, 1):
        for sz in (-1, 0, 1):
            position = 9 * (sx + 1) + 3 * (sy + 1) + (sz + 1)
            if position == 13:
                slot = mine + b
            else:
                slot = near[mine + b, position if position < 13 else position - 1]
            if sx == 0:
                plane = jnp.where((slot < 0) | (slot > 7), 64, 8 * slot + xp - 1)
            else:
                plane = jnp.where(slot < 0, 16, slot)
            loaded[sy, sz] = planes[plane].astype(F32).reshape(4, 16, 128)

    def merged(oy, sz, tile):
        inner = loaded[0, sz][tile]
        if oy == 0:
            return inner
        return jnp.where(qy == (3 if oy < 0 else 0), loaded[oy, sz][tile], inner)

    def turned(value, shift):
        return value if shift % 16 == 0 else pltpu.roll(value, shift % 16, 0)

    for i in range(4):
        for j in range(4):
            oy = (-1, 0, 0, 1)[i]
            oz = (-1, 0, 0, 1)[j]
            tile = (1, 0, 1, 0)[i] * 2 + (1, 0, 1, 0)[j]
            value = turned(merged(oy, 0, tile), -4 * oy - oz)
            if oz != 0:
                edge = turned(merged(oy, oz, tile), -4 * oy + 3 * oz)
                value = jnp.where(qz == (0 if oz < 0 else 3), edge, value)
            value = value.astype(BF16)
            for p in range(2):
                for e in range(2):
                    dy, dz = i - p, j - e
                    if 0 <= dy <= 2 and 0 <= dz <= 2:
                        row = 32 * p + 16 * e
                        col = 128 * (3 * dy + dz)
                        windows[b, xp, row : row + 16, col : col + 128] = value


def grid_of(peers):
    chips = peers // 2
    across = 4 if chips == 16 else (2 if chips == 4 else 1)
    return chips // across, across


class Links:
    def __init__(self):
        self.ny, self.nx = grid_of(lax.axis_size("space"))
        self.nz = lax.axis_size("chan")
        space = lax.axis_index("space")
        self.space = space
        self.z = lax.axis_index("chan")
        self.core = lax.rem(space, 2)
        self.x = lax.rem(space // 2, self.nx)
        self.y = space // (2 * self.nx)

    def device(self, y=None, x=None, z=None, core=None):
        y = self.y if y is None else y
        x = self.x if x is None else x
        z = self.z if z is None else z
        core = self.core if core is None else core
        return ((y * self.nx + x) * 2 + core, z)


def send(source, target, sems, device):
    pltpu.make_async_remote_copy(
        src_ref=source, dst_ref=target, send_sem=sems[0], recv_sem=sems[1],
        device_id=device, device_id_type=pl.DeviceIdType.MESH,
    ).start()


def arrived(ref, sems, device):
    pltpu.make_async_remote_copy(
        src_ref=ref, dst_ref=ref, send_sem=sems[0], recv_sem=sems[1],
        device_id=device, device_id_type=pl.DeviceIdType.MESH,
    ).wait_recv()


def left(ref, sems, device):
    pltpu.make_async_remote_copy(
        src_ref=ref, dst_ref=ref, send_sem=sems[0], recv_sem=sems[1],
        device_id=device, device_id_type=pl.DeviceIdType.MESH,
    ).wait_send()


def shifted(place, step, count):
    return lax.rem(place + step, count)


HALF = (256, 128, 128, 256)
FULL = (256, 128, 128, 192)
LEAD = ("z", "x", "y", "z")
CONV_ROWS = [(3, 32 * k + (64 if k > 5 else 0)) for k in range(11)]
CONV_ROWS += [(1, 32 * k) for k in range(8)] + [(2, 32 * k) for k in range(8)]


def group_of(color, ny, nx, nz):
    return {
        "z": (("y", ny), ("x", nx)), "x": (("z", nz), ("y", ny)), "y": (("z", nz), ("x", nx)),
    }[LEAD[color]]


class Reduce:
    def __init__(self, links, grads, pair, first, rest, second, sums, sems):
        self.k = links
        self.grads, self.pair, self.first, self.rest = grads, pair, first, rest
        self.second, self.sums, self.sems = second, sums, sems
        self.partner = links.device(core=1 - links.core)
        k = links
        self.counts = {"z": k.nz, "x": k.nx, "y": k.ny}
        self.minor = [group_of(color, k.ny, k.nx, k.nz) for color in range(4)]
        self.cell = [half // (k.nx * k.ny) for half in HALF]

    def at(self, name):
        return getattr(self.k, name)

    def sem(self, phase, color):
        return (self.sems.at[0, phase, color], self.sems.at[1, phase, color])

    def start_pair(self, color):
        away = pl.multiple_of(HALF[color] * (1 - self.k.core), 128)
        send(
            self.grads.at[color, :, pl.ds(away, FULL[color])],
            self.pair.at[color, :, 0 : FULL[color]], self.sem(0, color), self.partner,
        )

    def part(self, color, place):
        base = HALF[color] * self.k.core
        if LEAD[color] == "z":
            return place, pl.ds(pl.multiple_of(base, 128), FULL[color])
        rows = HALF[color] // self.counts[LEAD[color]]
        return slice(None), pl.ds(pl.multiple_of(base + place * rows, rows), rows)

    def start_major(self, color):
        full = FULL[color]
        rows = pl.ds(pl.multiple_of(HALF[color] * self.k.core, 128), full)
        arrived(self.pair.at[color, :, 0:full], self.sem(0, color), self.partner)
        for z in range(self.k.nz):
            self.grads[color, z, rows] += self.pair[color, z, 0:full]
        name = LEAD[color]
        count = self.counts[name]
        for step in range(1, count):
            place = shifted(self.at(name), step, count)
            chunk, span = self.part(color, place)
            send(
                self.grads.at[color, chunk, span], self.first[color].at[step - 1],
                self.sem(1, color), self.k.device(**{name: place}),
            )

    def start_minor(self, color):
        name = LEAD[color]
        count = self.counts[name]
        if count > 1:
            arrived(self.first[color].at[0 : count - 1], self.sem(1, color), self.partner)
        chunk, span = self.part(color, self.at(name))
        total = self.grads[color, chunk, span]
        for step in range(count - 1):
            total = total + self.first[color][step]
        cell = self.cell[color]
        used = FULL[color] // cell
        if LEAD[color] != "z":
            used = self.rest[color].shape[0]
        self.rest[color][0:used] = total.reshape(used, cell, 128)
        (n0, c0), (n1, c1) = self.minor[color]
        for step0 in range(c0):
            for step1 in range(c1):
                if step0 == 0 and step1 == 0:
                    continue
                p0 = shifted(self.at(n0), step0, c0)
                p1 = shifted(self.at(n1), step1, c1)
                send(
                    self.rest[color].at[p0 * c1 + p1],
                    self.second[color].at[step0 * c1 + step1 - 1],
                    self.sem(2, color), self.k.device(**{n0: p0, n1: p1}),
                )

    def home(self, color):
        k = self.k
        inner = (k.x * k.ny + k.y) if LEAD[color] == "x" else (k.y * k.nx + k.x)
        cell = self.cell[color]
        return pl.ds(pl.multiple_of(HALF[color] * k.core + inner * cell, cell), cell)

    def start_spread(self, color):
        k = self.k
        (n0, c0), (n1, c1) = self.minor[color]
        if c0 * c1 > 1:
            arrived(self.second[color], self.sem(2, color), self.partner)
        total = self.rest[color][self.at(n0) * c1 + self.at(n1)]
        for step in range(c0 * c1 - 1):
            total = total + self.second[color][step]
        self.sums[color, self.home(color)] = total
        for step0 in range(k.ny):
            for step1 in range(k.nx):
                if step0 == 0 and step1 == 0:
                    continue
                y = shifted(k.y, step0, k.ny)
                x = shifted(k.x, step1, k.nx)
                mine = self.sums.at[color, self.home(color)]
                send(mine, mine, self.sem(3, color), k.device(y=y, x=x))

    def others(self, color):
        return self.sums.at[color, 0 : (self.k.nx * self.k.ny - 1) * self.cell[color]]

    def start_share(self, color):
        if self.k.nx * self.k.ny > 1:
            arrived(self.others(color), self.sem(3, color), self.partner)
        half = HALF[color]
        mine = self.sums.at[color, pl.ds(pl.multiple_of(half * self.k.core, 128), half)]
        send(mine, mine, self.sem(4, color), self.partner)

    def finish(self, color):
        half = self.sums.at[color, 0 : HALF[color]]
        arrived(half, self.sem(4, color), self.partner)
        left(self.pair.at[color, :, 0 : FULL[color]], self.sem(0, color), self.partner)
        count = self.counts[LEAD[color]]
        if count > 1:
            left(self.first[color].at[0 : count - 1], self.sem(1, color), self.partner)
        if self.minor[color][0][1] * self.minor[color][1][1] > 1:
            left(self.second[color], self.sem(2, color), self.partner)
        if self.k.nx * self.k.ny > 1:
            left(self.others(color), self.sem(3, color), self.partner)
        left(half, self.sem(4, color), self.partner)


def reduce_scratch(peers, nz):
    ny, nx = grid_of(peers)
    counts = {"z": nz, "x": nx, "y": ny}
    first, rest, second = [], [], []
    for color in range(4):
        count = counts[LEAD[color]]
        if LEAD[color] == "z":
            shape = (max(count - 1, 1), FULL[color], 128)
        else:
            shape = (max(count - 1, 1), nz, HALF[color] // count, 128)
        first.append(pltpu.VMEM(shape, F32))
        (_, c0), (_, c1) = group_of(color, ny, nx, nz)
        cell = HALF[color] // (nx * ny)
        rest.append(pltpu.VMEM((c0 * c1, cell, 128), F32))
        second.append(pltpu.VMEM((max(c0 * c1 - 1, 1), cell, 128), F32))
    return [
        pltpu.VMEM((4, nz, 512, 128), F32), pltpu.VMEM((4, nz, 256, 128), F32),
        *first, *rest, *second,
        pltpu.VMEM((4, 512, 128), F32), pltpu.SemaphoreType.DMA((2, 5, 4)),
    ]


def signal_all(links):
    barrier = pltpu.get_barrier_semaphore()
    k = links
    targets = []
    for step in range(1, k.nz):
        z = shifted(k.z, step, k.nz)
        for other in range(k.ny):
            targets.append(k.device(y=shifted(k.y, other, k.ny), z=z))
        for other in range(1, k.nx):
            targets.append(k.device(x=shifted(k.x, other, k.nx), z=z))
    for step in range(1, k.ny * k.nx * 2):
        targets.append((shifted(k.space, step, k.ny * k.nx * 2), k.z))
    for target in targets:
        pl.semaphore_signal(
            barrier, inc=1, device_id=target, device_id_type=pl.DeviceIdType.MESH
        )
    return barrier, len(targets)


def start_exchange(links, source, target, sems):
    peers = links.ny * links.nx * 2
    for step in range(1, peers):
        place = shifted(links.space, step, peers)
        send(source.at[place], target.at[links.space], sems, (place, links.z))
    target[links.space] = source[links.space]


def start_columns(links, source, target, sems):
    for step in range(1, links.nz):
        place = shifted(links.z, step, links.nz)
        send(source.at[place], target.at[links.z], sems, (links.space, place))
    target[links.z] = source[links.z]


def step_kernel(
    near, owner, features_hbm, mask_hbm, w_conv_hbm, w_down_hbm, cotangent_hbm,
    coarse_pairs_ref, conv_ref, down_ref,
    features, mask, w_own, w_down, cotangent, w_conv,
    table, rims, windows, octants, factor, slopes, row_mask,
    cot_out, cot_in, piece_out, piece_in, dpiece_out, dpiece_in,
    halves, coarse_out, coarse_in, local_sems, front_sems,
    grads, pair, first_0, first_1, first_2, first_3, rest_0, rest_1, rest_2, rest_3,
    second_0, second_1, second_2, second_3, sums, sems,
):
    links = Links()
    peers = links.ny * links.nx * 2
    nz = links.nz
    partner = links.device(core=1 - links.core)
    mine = links.z * 2
    reduce = Reduce(
        links, grads, pair, (first_0, first_1, first_2, first_3),
        (rest_0, rest_1, rest_2, rest_3), (second_0, second_1, second_2, second_3), sums, sems,
    )

    def front(n):
        return (front_sems.at[0, n], front_sems.at[1, n])

    def pass_on(dx):
        for step in range(1, nz):
            z = shifted(links.z, nz - step, nz)
            rows = pl.ds(pl.multiple_of(32 * z + 16 * links.core, 16), 16)
            piece = w_conv.at[dx, rows]
            arrived(piece, front(10 + 3 * step + dx - 3), partner)
            send(piece, piece, front(19 + dx), partner)

    loads = [
        pltpu.make_async_copy(source, target, local_sems.at[n])
        for n, (source, target) in enumerate(
            (
                (w_conv_hbm, w_own), (cotangent_hbm, cotangent), (mask_hbm, mask),
                (features_hbm, features), (w_down_hbm, w_down),
            )
        )
    ]
    for load in loads:
        load.start()
    barrier, signals = signal_all(links)
    order = voxel_order()

    table[64] = jnp.zeros((64, 128), BF16)
    rims[0, 12:17] = jnp.zeros((5, 64, 128), BF16)
    rims[1, 8:12] = jnp.zeros((4, 64, 128), BF16)
    rims[1, 16] = jnp.zeros((64, 128), BF16)
    for z in range(nz):
        grads[3, z, 416:448] = jnp.zeros((32, 128), F32)
    rest_3[...] = jnp.zeros_like(rest_3)
    for r in range(2):
        halves[r, 8] = jnp.zeros((64, 128), BF16)
    loads[0].wait()
    for k in range(27):
        dx, d = k // 9, k % 9
        rows = pl.ds(pl.multiple_of(32 * links.z, 32), 32)
        w_conv[dx, rows, 128 * d : 128 * d + 128] = w_own[k]
    loads[1].wait()

    @pl.loop(0, peers)
    def _(d):
        cot_out[d, :, 0:64] = cotangent[2 * d]
        cot_out[d, :, 64:128] = cotangent[2 * d + 1]

    pl.semaphore_wait(barrier, signals)
    own_rows = pl.ds(pl.multiple_of(32 * links.z + 16 * links.core, 16), 16)
    for dx in range(3):
        for step in range(1, nz):
            z = shifted(links.z, step, nz)
            piece = w_conv.at[dx, own_rows]
            send(piece, piece, front(10 + 3 * step + dx - 3), links.device(z=z))

    loads[2].wait()
    loads[3].wait()

    @pl.loop(0, 8)
    def _(g):
        keep = mask[pl.ds(g, 1), :].astype(F32).astype(BF16)
        masked = features[g] * keep
        for h in range(2):
            turned = lax.dot_general(
                order, masked[:, 256 * h : 256 * h + 256], NT, preferred_element_type=F32
            )
            table[pl.ds(8 * g + 4 * h, 4)] = turned.astype(BF16).reshape(4, 64, 128)

    following = (shifted(links.space, 1, peers), links.z)
    previous = (shifted(links.space, peers - 1, peers), links.z)
    for j in range(8):
        rims[0, j] = table[8 * j + 7]
        rims[1, j] = table[8 * j]
    send(rims.at[0, 4:8], rims.at[0, 8:12], front(1), following)
    send(rims.at[1, 0:4], rims.at[1, 12:16], front(2), previous)
    start_exchange(links, cot_out, cot_in, front(0))
    for b in range(2):
        keep = mask[pl.ds(mine + b, 1), :].astype(F32)
        for h in range(2):
            wide = jnp.broadcast_to(keep[:, 256 * h : 256 * h + 256], (128, 256)).astype(BF16)
            turned = lax.dot_general(order, wide, NT, preferred_element_type=F32)
            row_mask[b, 256 * h : 256 * h + 256, :] = turned

        @pl.loop(1, 9)
        def _(xp):
            fill_plane(windows, table, near, b, mine, xp, 0)

    pass_on(0)
    arrived(rims.at[0, 8:12], front(1), previous)
    arrived(rims.at[1, 12:16], front(2), following)

    @pl.when(links.space == 0)
    def _():
        rims[0, 8:12] = jnp.zeros((4, 64, 128), BF16)

    @pl.when(links.space == peers - 1)
    def _():
        rims[1, 12:16] = jnp.zeros((4, 64, 128), BF16)

    for b in range(2):
        fill_plane(windows, rims.at[0], near, b, mine, 0, -1)
        fill_plane(windows, rims.at[1], near, b, mine, 9, 1)
    for dx in range(3):
        if dx < 2:
            pass_on(dx + 1)
        else:
            arrived(cot_in.at[0 : peers - 1], front(0), partner)
            owners = [owner[0, g] for g in range(8)]
            low = lax.broadcasted_iota(jnp.int32, (64, 128), 1) < 64
            for z in range(4):
                parts = []
                for i in range(2):
                    g = 2 * z + i
                    rank = jnp.int32(0)
                    for h in range(g):
                        rank = rank + jnp.where(owners[h] == owners[g], 1, 0)
                    value = cot_in[owners[g]].astype(F32)
                    parts.append(jnp.where(rank == i, value, pltpu.roll(value, 64, 1)))
                dpiece_out[z] = jnp.where(low, parts[0], parts[1]).astype(BF16)
            start_columns(links, dpiece_out, dpiece_in, front(5))

        arrived(w_conv.at[dx, 0 : 16 * (nz - 1)], front(19 + dx), partner)
        for b in range(2):
            part = lax.dot_general(
                windows[b, dx : dx + 8].reshape(512, 1152), w_conv[dx], NT,
                preferred_element_type=F32,
            )
            if dx == 0:
                slopes[b] = part
            else:
                slopes[b] += part
    for b in range(2):
        own = table[pl.ds(8 * (mine + b), 8)].astype(F32).reshape(512, 128)
        pre = own + slopes[b]
        keep = row_mask[b]
        gate = jax.nn.sigmoid(pre)
        hidden = (keep * (pre * gate)).astype(BF16).reshape(4, 2, 4, 16, 128)
        factor[b] = keep * gate * (1.0 + pre * (1.0 - gate))
        for a in range(2):
            for t in range(4):
                octants[4 * a + t, 64 * b : 64 * b + 64, :] = hidden[:, a, t].reshape(64, 128)
    loads[4].wait()
    total = None
    for o in range(8):
        part = lax.dot_general(w_down[o], octants[o], NT, preferred_element_type=F32)
        total = part if total is None else total + part
    piece_out[...] = total.astype(BF16).reshape(nz, 64, 128)
    start_columns(links, piece_out, piece_in, front(4))

    arrived(dpiece_in.at[0 : nz - 1], front(5), partner)
    piece = dpiece_in[...].reshape(256, 128)
    piece_rows = piece.astype(F32).T.astype(BF16)
    for o in range(8):
        part = jnp.dot(piece, octants[o], preferred_element_type=F32)
        for z in range(4):
            grads[0, z, 64 * o : 64 * o + 64, :] = part[64 * z : 64 * z + 64]
    reduce.start_pair(0)
    for b in range(2):
        for a in range(2):
            for t in range(4):
                o = 4 * a + t
                dhidden = jnp.dot(
                    piece_rows[64 * b : 64 * b + 64], w_down[o], preferred_element_type=F32
                ).reshape(4, 16, 128)
                for qx in range(4):
                    row = 64 * (2 * qx + a) + 16 * t
                    slopes[b, row : row + 16, :] = dhidden[qx] * factor[b, row : row + 16, :]
    arrived(piece_in.at[0 : nz - 1], front(4), partner)
    for g in range(8):
        value = piece_in[g // 2].astype(F32)
        swapped = pltpu.roll(value, 64, 1)
        first, other = (value, swapped) if g % 2 == 0 else (swapped, value)
        halves[0, g] = jnp.where(low, first, 0.0).astype(BF16)
        halves[1, g] = jnp.where(low, 0.0, other).astype(BF16)

    @pl.loop(0, peers)
    def _(d):
        place_0 = jnp.int32(8)
        place_1 = jnp.int32(8)
        for g in range(7, -1, -1):
            hit = owners[g] == d
            place_1 = jnp.where(hit, place_0, place_1)
            place_0 = jnp.where(hit, g, place_0)
        coarse_out[d] = halves[0, place_0] + halves[1, place_1]

    start_exchange(links, coarse_out, coarse_in, front(9))

    turned = [slopes[b].astype(BF16).astype(F32).T.astype(BF16) for b in range(2)]
    for dx in range(3):
        total = None
        for b in range(2):
            part = jnp.dot(
                turned[b], windows[b, dx : dx + 8].reshape(512, 1152), preferred_element_type=F32
            )
            total = part if total is None else total + part
        for d in range(9):
            k = 9 * dx + d
            color, row = CONV_ROWS[k]
            for z in range(4):
                grads[color, z, row : row + 32, :] = total[
                    32 * z : 32 * z + 32, 128 * d : 128 * d + 128
                ]
        if dx == 0:
            reduce.start_major(0)
        elif dx == 1:
            reduce.start_pair(3)
    reduce.start_pair(1)
    reduce.start_pair(2)
    reduce.start_major(3)
    reduce.start_major(1)
    reduce.start_major(2)
    for color in (0, 1, 2, 3):
        reduce.start_minor(color)
    for color in (0, 1, 2, 3):
        reduce.start_spread(color)

    arrived(coarse_in.at[0 : peers - 1], front(9), partner)

    coarse_pairs_ref[...] = coarse_in[...]
    for color in (0, 1, 2, 3):
        reduce.start_share(color)
    for color in range(4):
        reduce.finish(color)
        if color == 0:
            for o in range(8):
                down_ref[o] = sums[0, 64 * o : 64 * o + 64]
        for k in range(27):
            if CONV_ROWS[k][0] == color:
                conv_ref[k] = sums[color, CONV_ROWS[k][1] : CONV_ROWS[k][1] + 32]
    left(cot_out.at[0 : peers - 1], front(0), partner)
    left(rims.at[0, 4:8], front(1), partner)
    left(rims.at[1, 0:4], front(2), partner)
    left(piece_out.at[0 : nz - 1], front(4), partner)
    left(dpiece_out.at[0 : nz - 1], front(5), partner)
    for dx in range(3):
        left(w_conv.at[dx, 0 : 16 * (nz - 1)], front(19 + dx), partner)
        for step in range(1, nz):
            left(w_conv.at[dx, 0:16], front(10 + 3 * step + dx - 3), partner)
    left(coarse_out.at[0 : peers - 1], front(9), partner)


def finish_kernel(pairs, conv, down, coarse_out, conv_out, down_out, coarse, sems):
    quarter = pairs.shape[0] // 4
    stores = [
        pltpu.make_async_copy(conv, conv_out, sems.at[4]),
        pltpu.make_async_copy(down, down_out, sems.at[5]),
    ]
    for store in stores:
        store.start()
    for n in range(4):
        for d in range(n * quarter, (n + 1) * quarter):
            coarse[2 * d] = pairs[d, :, 0:64]
            coarse[2 * d + 1] = pairs[d, :, 64:128]
        store = pltpu.make_async_copy(
            coarse.at[2 * n * quarter : 2 * (n + 1) * quarter],
            coarse_out.at[2 * n * quarter : 2 * (n + 1) * quarter], sems.at[n],
        )
        store.start()
        stores.append(store)
    for store in stores:
        store.wait()


def local(features, voxel_mask, neighbors, w_conv, w_down, coarse_owner, cotangent):
    peers = lax.axis_size("space")
    nz = lax.axis_size("chan")
    smem = pl.BlockSpec(memory_space=pltpu.SMEM)
    vmem = pl.BlockSpec(memory_space=pltpu.VMEM)
    anywhere = pl.BlockSpec(memory_space=pl.ANY)
    coarse_pairs, conv_sum, down_sum = pl.pallas_call(
        step_kernel,
        out_shape=(
            pltpu.VMEM((peers, 64, 128), BF16),
            pltpu.VMEM((27, 32, 128), F32),
            pltpu.VMEM((8, 64, 128), F32),
        ),
        in_specs=[smem, smem] + [anywhere] * 5,
        out_specs=(vmem, vmem, vmem),
        scratch_shapes=[
            pltpu.VMEM((8, 128, 512), BF16),
            pltpu.VMEM((8, 512), jnp.int32),
            pltpu.VMEM((27, 32, 128), BF16),
            pltpu.VMEM((8, 256, 128), BF16),
            pltpu.VMEM(cotangent.shape, BF16),
            pltpu.VMEM((3, 128, 1152), BF16),
            pltpu.VMEM((65, 64, 128), BF16),
            pltpu.VMEM((2, 17, 64, 128), BF16),
            pltpu.VMEM((2, 10, 64, 1152), BF16),
            pltpu.VMEM((8, 128, 128), BF16),
            pltpu.VMEM((2, 512, 128), F32),
            pltpu.VMEM((2, 512, 128), F32),
            pltpu.VMEM((2, 512, 128), F32),
            pltpu.VMEM((peers, 64, 128), BF16),
            pltpu.VMEM((peers, 64, 128), BF16),
            pltpu.VMEM((nz, 64, 128), BF16),
            pltpu.VMEM((nz, 64, 128), BF16),
            pltpu.VMEM((nz, 64, 128), BF16),
            pltpu.VMEM((nz, 64, 128), BF16),
            pltpu.VMEM((2, 9, 64, 128), BF16),
            pltpu.VMEM((peers, 64, 128), BF16),
            pltpu.VMEM((peers, 64, 128), BF16),
            pltpu.SemaphoreType.DMA((8,)),
            pltpu.SemaphoreType.DMA((2, 22)),
        ]
        + reduce_scratch(peers, nz),
        compiler_params=pltpu.CompilerParams(
            vmem_limit_bytes=56 << 20, collective_id=0, has_side_effects=True
        ),
    )(neighbors, coarse_owner.reshape(1, 8), features, voxel_mask, w_conv, w_down, cotangent)
    return pl.pallas_call(
        finish_kernel,
        out_shape=(
            jax.ShapeDtypeStruct(cotangent.shape, BF16),
            jax.ShapeDtypeStruct((27, 32, 128), F32),
            jax.ShapeDtypeStruct((8, 64, 128), F32),
        ),
        in_specs=[vmem] * 3,
        out_specs=(anywhere,) * 3,
        scratch_shapes=[
            pltpu.VMEM(cotangent.shape, BF16), pltpu.SemaphoreType.DMA((6,)),
        ],
    )(
        *(
            pltpu.with_memory_space_constraint(value, pltpu.VMEM)
            for value in (coarse_pairs, conv_sum, down_sum)
        )
    )


def solution(mesh):
    in_specs = (
        P("space", None, None),
        P("space", None),
        P("space", None),
        P(None, "chan", None),
        P(),
        P("space", None),
        P("space", "chan", None),
    )
    out_specs = (P("space", "chan", None), P(None, "chan", None), P(None, "chan", None))
    return jax.shard_map(local, mesh=mesh, in_specs=in_specs, out_specs=out_specs, check_vma=False)
```

```python
import jax
import jax.numpy as jnp
from jax import lax
from jax.experimental import pallas as pl
from jax.experimental.pallas import tpu as pltpu
from jax.sharding import PartitionSpec as P

F32 = jnp.float32
BF16 = jnp.bfloat16
NT = (((1,), (1,)), ((), ()))


def voxel_order():
    row = lax.broadcasted_iota(jnp.int32, (256, 256), 0)
    col = lax.broadcasted_iota(jnp.int32, (256, 256), 1)
    y = ((row >> 2) & 3) * 2 + ((row >> 5) & 1)
    z = (row & 3) * 2 + ((row >> 4) & 1)
    source = (row & ~63) + y * 8 + z
    return (source == col).astype(F32).astype(BF16)


def fill_plane(windows, planes, near, b, mine, xp, sx):
    qy = (lax.broadcasted_iota(jnp.int32, (16, 128), 0) >> 2) & 3
    qz = lax.broadcasted_iota(jnp.int32, (16, 128), 0) & 3
    loaded = {}
    for sy in (-1, 0, 1):
        for sz in (-1, 0, 1):
            position = 9 * (sx + 1) + 3 * (sy + 1) + (sz + 1)
            if position == 13:
                slot = mine + b
            else:
                slot = near[mine + b, position if position < 13 else position - 1]
            if sx == 0:
                plane = jnp.where((slot < 0) | (slot > 7), 64, 8 * slot + xp - 1)
            else:
                plane = jnp.where(slot < 0, 16, slot)
            loaded[sy, sz] = planes[plane].astype(F32).reshape(4, 16, 128)

    def merged(oy, sz, tile):
        inner = loaded[0, sz][tile]
        if oy == 0:
            return inner
        return jnp.where(qy == (3 if oy < 0 else 0), loaded[oy, sz][tile], inner)

    def turned(value, shift):
        return value if shift % 16 == 0 else pltpu.roll(value, shift % 16, 0)

    for i in range(4):
        for j in range(4):
            oy = (-1, 0, 0, 1)[i]
            oz = (-1, 0, 0, 1)[j]
            tile = (1, 0, 1, 0)[i] * 2 + (1, 0, 1, 0)[j]
            value = turned(merged(oy, 0, tile), -4 * oy - oz)
            if oz != 0:
                edge = turned(merged(oy, oz, tile), -4 * oy + 3 * oz)
                value = jnp.where(qz == (0 if oz < 0 else 3), edge, value)
            value = value.astype(BF16)
            for p in range(2):
                for e in range(2):
                    dy, dz = i - p, j - e
                    if 0 <= dy <= 2 and 0 <= dz <= 2:
                        row = 32 * p + 16 * e
                        col = 128 * (3 * dy + dz)
                        windows[b, xp, row : row + 16, col : col + 128] = value


def grid_of(peers):
    chips = peers // 2
    across = 4 if chips == 16 else (2 if chips == 4 else 1)
    return chips // across, across


class Links:
    def __init__(self):
        self.ny, self.nx = grid_of(lax.axis_size("space"))
        self.nz = lax.axis_size("chan")
        space = lax.axis_index("space")
        self.space = space
        self.z = lax.axis_index("chan")
        self.core = lax.rem(space, 2)
        self.x = lax.rem(space // 2, self.nx)
        self.y = space // (2 * self.nx)

    def device(self, y=None, x=None, z=None, core=None):
        y = self.y if y is None else y
        x = self.x if x is None else x
        z = self.z if z is None else z
        core = self.core if core is None else core
        return ((y * self.nx + x) * 2 + core, z)


def send(source, target, sems, device):
    pltpu.make_async_remote_copy(
        src_ref=source, dst_ref=target, send_sem=sems[0], recv_sem=sems[1],
        device_id=device, device_id_type=pl.DeviceIdType.MESH,
    ).start()


def arrived(ref, sems, device):
    pltpu.make_async_remote_copy(
        src_ref=ref, dst_ref=ref, send_sem=sems[0], recv_sem=sems[1],
        device_id=device, device_id_type=pl.DeviceIdType.MESH,
    ).wait_recv()


def left(ref, sems, device):
    pltpu.make_async_remote_copy(
        src_ref=ref, dst_ref=ref, send_sem=sems[0], recv_sem=sems[1],
        device_id=device, device_id_type=pl.DeviceIdType.MESH,
    ).wait_send()


def shifted(place, step, count):
    return lax.rem(place + step, count)


HALF = (256, 128, 128, 256)
FULL = (256, 128, 128, 192)
LEAD = ("z", "x", "y", "z")
CONV_ROWS = [(3, 32 * k + (64 if k > 5 else 0)) for k in range(11)]
CONV_ROWS += [(1, 32 * k) for k in range(8)] + [(2, 32 * k) for k in range(8)]


def group_of(color, ny, nx, nz):
    return {
        "z": (("y", ny), ("x", nx)), "x": (("z", nz), ("y", ny)), "y": (("z", nz), ("x", nx)),
    }[LEAD[color]]


class Reduce:
    def __init__(self, links, grads, pair, first, rest, second, sums, sems):
        self.k = links
        self.grads, self.pair, self.first, self.rest = grads, pair, first, rest
        self.second, self.sums, self.sems = second, sums, sems
        self.partner = links.device(core=1 - links.core)
        k = links
        self.counts = {"z": k.nz, "x": k.nx, "y": k.ny}
        self.minor = [group_of(color, k.ny, k.nx, k.nz) for color in range(4)]
        self.cell = [half // (k.nx * k.ny) for half in HALF]

    def at(self, name):
        return getattr(self.k, name)

    def sem(self, phase, color):
        return (self.sems.at[0, phase, color], self.sems.at[1, phase, color])

    def start_pair(self, color):
        away = pl.multiple_of(HALF[color] * (1 - self.k.core), 128)
        send(
            self.grads.at[color, :, pl.ds(away, FULL[color])],
            self.pair.at[color, :, 0 : FULL[color]], self.sem(0, color), self.partner,
        )

    def part(self, color, place):
        base = HALF[color] * self.k.core
        if LEAD[color] == "z":
            return place, pl.ds(pl.multiple_of(base, 128), FULL[color])
        rows = HALF[color] // self.counts[LEAD[color]]
        return slice(None), pl.ds(pl.multiple_of(base + place * rows, rows), rows)

    def start_major(self, color):
        full = FULL[color]
        rows = pl.ds(pl.multiple_of(HALF[color] * self.k.core, 128), full)
        arrived(self.pair.at[color, :, 0:full], self.sem(0, color), self.partner)
        for z in range(self.k.nz):
            self.grads[color, z, rows] += self.pair[color, z, 0:full]
        name = LEAD[color]
        count = self.counts[name]
        for step in range(1, count):
            place = shifted(self.at(name), step, count)
            chunk, span = self.part(color, place)
            send(
                self.grads.at[color, chunk, span], self.first[color].at[step - 1],
                self.sem(1, color), self.k.device(**{name: place}),
            )

    def start_minor(self, color):
        name = LEAD[color]
        count = self.counts[name]
        if count > 1:
            arrived(self.first[color].at[0 : count - 1], self.sem(1, color), self.partner)
        chunk, span = self.part(color, self.at(name))
        total = self.grads[color, chunk, span]
        for step in range(count - 1):
            total = total + self.first[color][step]
        cell = self.cell[color]
        used = FULL[color] // cell
        if LEAD[color] != "z":
            used = self.rest[color].shape[0]
        self.rest[color][0:used] = total.reshape(used, cell, 128)
        (n0, c0), (n1, c1) = self.minor[color]
        for step0 in range(c0):
            for step1 in range(c1):
                if step0 == 0 and step1 == 0:
                    continue
                p0 = shifted(self.at(n0), step0, c0)
                p1 = shifted(self.at(n1), step1, c1)
                send(
                    self.rest[color].at[p0 * c1 + p1],
                    self.second[color].at[step0 * c1 + step1 - 1],
                    self.sem(2, color), self.k.device(**{n0: p0, n1: p1}),
                )

    def home(self, color):
        k = self.k
        inner = (k.x * k.ny + k.y) if LEAD[color] == "x" else (k.y * k.nx + k.x)
        cell = self.cell[color]
        return pl.ds(pl.multiple_of(HALF[color] * k.core + inner * cell, cell), cell)

    def start_spread(self, color):
        k = self.k
        (n0, c0), (n1, c1) = self.minor[color]
        if c0 * c1 > 1:
            arrived(self.second[color], self.sem(2, color), self.partner)
        total = self.rest[color][self.at(n0) * c1 + self.at(n1)]
        for step in range(c0 * c1 - 1):
            total = total + self.second[color][step]
        self.sums[color, self.home(color)] = total
        for step0 in range(k.ny):
            for step1 in range(k.nx):
                if step0 == 0 and step1 == 0:
                    continue
                y = shifted(k.y, step0, k.ny)
                x = shifted(k.x, step1, k.nx)
                mine = self.sums.at[color, self.home(color)]
                send(mine, mine, self.sem(3, color), k.device(y=y, x=x))

    def others(self, color):
        return self.sums.at[color, 0 : (self.k.nx * self.k.ny - 1) * self.cell[color]]

    def start_share(self, color):
        if self.k.nx * self.k.ny > 1:
            arrived(self.others(color), self.sem(3, color), self.partner)
        half = HALF[color]
        mine = self.sums.at[color, pl.ds(pl.multiple_of(half * self.k.core, 128), half)]
        send(mine, mine, self.sem(4, color), self.partner)

    def finish(self, color):
        half = self.sums.at[color, 0 : HALF[color]]
        arrived(half, self.sem(4, color), self.partner)
        left(self.pair.at[color, :, 0 : FULL[color]], self.sem(0, color), self.partner)
        count = self.counts[LEAD[color]]
        if count > 1:
            left(self.first[color].at[0 : count - 1], self.sem(1, color), self.partner)
        if self.minor[color][0][1] * self.minor[color][1][1] > 1:
            left(self.second[color], self.sem(2, color), self.partner)
        if self.k.nx * self.k.ny > 1:
            left(self.others(color), self.sem(3, color), self.partner)
        left(half, self.sem(4, color), self.partner)


def reduce_scratch(peers, nz):
    ny, nx = grid_of(peers)
    counts = {"z": nz, "x": nx, "y": ny}
    first, rest, second = [], [], []
    for color in range(4):
        count = counts[LEAD[color]]
        if LEAD[color] == "z":
            shape = (max(count - 1, 1), FULL[color], 128)
        else:
            shape = (max(count - 1, 1), nz, HALF[color] // count, 128)
        first.append(pltpu.VMEM(shape, F32))
        (_, c0), (_, c1) = group_of(color, ny, nx, nz)
        cell = HALF[color] // (nx * ny)
        rest.append(pltpu.VMEM((c0 * c1, cell, 128), F32))
        second.append(pltpu.VMEM((max(c0 * c1 - 1, 1), cell, 128), F32))
    return [
        pltpu.VMEM((4, nz, 512, 128), F32), pltpu.VMEM((4, nz, 256, 128), F32),
        *first, *rest, *second,
        pltpu.VMEM((4, 512, 128), F32), pltpu.SemaphoreType.DMA((2, 5, 4)),
    ]


def signal_all(links):
    barrier = pltpu.get_barrier_semaphore()
    k = links
    targets = []
    for step in range(1, k.nz):
        z = shifted(k.z, step, k.nz)
        for other in range(k.ny):
            targets.append(k.device(y=shifted(k.y, other, k.ny), z=z))
        for other in range(1, k.nx):
            targets.append(k.device(x=shifted(k.x, other, k.nx), z=z))
    for step in range(1, k.ny * k.nx * 2):
        targets.append((shifted(k.space, step, k.ny * k.nx * 2), k.z))
    for target in targets:
        pl.semaphore_signal(
            barrier, inc=1, device_id=target, device_id_type=pl.DeviceIdType.MESH
        )
    return barrier, len(targets)


def start_exchange(links, source, target, sems):
    peers = links.ny * links.nx * 2
    for step in range(1, peers):
        place = shifted(links.space, step, peers)
        send(source.at[place], target.at[links.space], sems, (place, links.z))
    target[links.space] = source[links.space]


def start_columns(links, source, target, sems):
    for step in range(1, links.nz):
        place = shifted(links.z, step, links.nz)
        send(source.at[place], target.at[links.z], sems, (links.space, place))
    target[links.z] = source[links.z]


def step_kernel(
    near, owner, features_hbm, mask_hbm, w_conv_hbm, w_down_hbm, cotangent_hbm,
    coarse_pairs_ref, conv_ref, down_ref,
    features, mask, w_own, w_down, cotangent, w_conv,
    table, rims, windows, octants, factor, slopes, row_mask,
    cot_out, cot_in, piece_out, piece_in, dpiece_out, dpiece_in,
    halves, coarse_out, coarse_in, local_sems, front_sems,
    grads, pair, first_0, first_1, first_2, first_3, rest_0, rest_1, rest_2, rest_3,
    second_0, second_1, second_2, second_3, sums, sems,
):
    links = Links()
    peers = links.ny * links.nx * 2
    nz = links.nz
    partner = links.device(core=1 - links.core)
    mine = links.z * 2
    reduce = Reduce(
        links, grads, pair, (first_0, first_1, first_2, first_3),
        (rest_0, rest_1, rest_2, rest_3), (second_0, second_1, second_2, second_3), sums, sems,
    )

    def front(n):
        return (front_sems.at[0, n], front_sems.at[1, n])

    def pass_on(dx):
        for step in range(1, nz):
            z = shifted(links.z, nz - step, nz)
            rows = pl.ds(pl.multiple_of(32 * z + 16 * links.core, 16), 16)
            piece = w_conv.at[dx, rows]
            arrived(piece, front(10 + 3 * step + dx - 3), partner)
            send(piece, piece, front(19 + dx), partner)

    loads = [
        pltpu.make_async_copy(source, target, local_sems.at[n])
        for n, (source, target) in enumerate(
            (
                (w_conv_hbm, w_own), (cotangent_hbm, cotangent), (mask_hbm, mask),
                (features_hbm, features), (w_down_hbm, w_down),
            )
        )
    ]
    for load in loads:
        load.start()
    barrier, signals = signal_all(links)
    order = voxel_order()

    table[64] = jnp.zeros((64, 128), BF16)
    rims[0, 12:17] = jnp.zeros((5, 64, 128), BF16)
    rims[1, 8:12] = jnp.zeros((4, 64, 128), BF16)
    rims[1, 16] = jnp.zeros((64, 128), BF16)
    for z in range(nz):
        grads[3, z, 416:448] = jnp.zeros((32, 128), F32)
    rest_3[...] = jnp.zeros_like(rest_3)
    for r in range(2):
        halves[r, 8] = jnp.zeros((64, 128), BF16)
    loads[0].wait()
    for k in range(27):
        dx, d = k // 9, k % 9
        rows = pl.ds(pl.multiple_of(32 * links.z, 32), 32)
        w_conv[dx, rows, 128 * d : 128 * d + 128] = w_own[k]
    loads[1].wait()

    @pl.loop(0, peers)
    def _(d):
        cot_out[d, :, 0:64] = cotangent[2 * d]
        cot_out[d, :, 64:128] = cotangent[2 * d + 1]

    loads[2].wait()
    loads[3].wait()

    @pl.loop(0, 4)
    def _(g):
        keep = mask[pl.ds(g, 1), :].astype(F32).astype(BF16)
        masked = features[g] * keep
        for h in range(2):
            turned = lax.dot_general(
                order, masked[:, 256 * h : 256 * h + 256], NT, preferred_element_type=F32
            )
            table[pl.ds(8 * g + 4 * h, 4)] = turned.astype(BF16).reshape(4, 64, 128)

    pl.semaphore_wait(barrier, signals)
    own_rows = pl.ds(pl.multiple_of(32 * links.z + 16 * links.core, 16), 16)
    for dx in range(3):
        for step in range(1, nz):
            z = shifted(links.z, step, nz)
            piece = w_conv.at[dx, own_rows]
            send(piece, piece, front(10 + 3 * step + dx - 3), links.device(z=z))


    @pl.loop(4, 8)
    def _(g):
        keep = mask[pl.ds(g, 1), :].astype(F32).astype(BF16)
        masked = features[g] * keep
        for h in range(2):
            turned = lax.dot_general(
                order, masked[:, 256 * h : 256 * h + 256], NT, preferred_element_type=F32
            )
            table[pl.ds(8 * g + 4 * h, 4)] = turned.astype(BF16).reshape(4, 64, 128)

    following = (shifted(links.space, 1, peers), links.z)
    previous = (shifted(links.space, peers - 1, peers), links.z)
    for j in range(8):
        rims[0, j] = table[8 * j + 7]
        rims[1, j] = table[8 * j]
    send(rims.at[0, 4:8], rims.at[0, 8:12], front(1), following)
    send(rims.at[1, 0:4], rims.at[1, 12:16], front(2), previous)
    start_exchange(links, cot_out, cot_in, front(0))
    for b in range(2):
        keep = mask[pl.ds(mine + b, 1), :].astype(F32)
        for h in range(2):
            wide = jnp.broadcast_to(keep[:, 256 * h : 256 * h + 256], (128, 256)).astype(BF16)
            turned = lax.dot_general(order, wide, NT, preferred_element_type=F32)
            row_mask[b, 256 * h : 256 * h + 256, :] = turned

        @pl.loop(1, 9)
        def _(xp):
            fill_plane(windows, table, near, b, mine, xp, 0)

    pass_on(0)
    arrived(rims.at[0, 8:12], front(1), previous)
    arrived(rims.at[1, 12:16], front(2), following)

    @pl.when(links.space == 0)
    def _():
        rims[0, 8:12] = jnp.zeros((4, 64, 128), BF16)

    @pl.when(links.space == peers - 1)
    def _():
        rims[1, 12:16] = jnp.zeros((4, 64, 128), BF16)

    for b in range(2):
        fill_plane(windows, rims.at[0], near, b, mine, 0, -1)
        fill_plane(windows, rims.at[1], near, b, mine, 9, 1)
    for dx in range(3):
        if dx < 2:
            pass_on(dx + 1)
        else:
            arrived(cot_in.at[0 : peers - 1], front(0), partner)
            owners = [owner[0, g] for g in range(8)]
            low = lax.broadcasted_iota(jnp.int32, (64, 128), 1) < 64
            for z in range(4):
                parts = []
                for i in range(2):
                    g = 2 * z + i
                    rank = jnp.int32(0)
                    for h in range(g):
                        rank = rank + jnp.where(owners[h] == owners[g], 1, 0)
                    value = cot_in[owners[g]].astype(F32)
                    parts.append(jnp.where(rank == i, value, pltpu.roll(value, 64, 1)))
                dpiece_out[z] = jnp.where(low, parts[0], parts[1]).astype(BF16)
            start_columns(links, dpiece_out, dpiece_in, front(5))

        arrived(w_conv.at[dx, 0 : 16 * (nz - 1)], front(19 + dx), partner)
        for b in range(2):
            part = lax.dot_general(
                windows[b, dx : dx + 8].reshape(512, 1152), w_conv[dx], NT,
                preferred_element_type=F32,
            )
            if dx == 0:
                slopes[b] = part
            else:
                slopes[b] += part
    for b in range(2):
        own = table[pl.ds(8 * (mine + b), 8)].astype(F32).reshape(512, 128)
        pre = own + slopes[b]
        keep = row_mask[b]
        gate = jax.nn.sigmoid(pre)
        hidden = (keep * (pre * gate)).astype(BF16).reshape(4, 2, 4, 16, 128)
        factor[b] = keep * gate * (1.0 + pre * (1.0 - gate))
        for a in range(2):
            for t in range(4):
                octants[4 * a + t, 64 * b : 64 * b + 64, :] = hidden[:, a, t].reshape(64, 128)
    loads[4].wait()
    total = None
    for o in range(8):
        part = lax.dot_general(w_down[o], octants[o], NT, preferred_element_type=F32)
        total = part if total is None else total + part
    piece_out[...] = total.astype(BF16).reshape(nz, 64, 128)
    start_columns(links, piece_out, piece_in, front(4))

    arrived(dpiece_in.at[0 : nz - 1], front(5), partner)
    piece = dpiece_in[...].reshape(256, 128)
    piece_rows = piece.astype(F32).T.astype(BF16)
    for o in range(8):
        part = jnp.dot(piece, octants[o], preferred_element_type=F32)
        for z in range(4):
            grads[0, z, 64 * o : 64 * o + 64, :] = part[64 * z : 64 * z + 64]
    reduce.start_pair(0)
    for b in range(2):
        for a in range(2):
            for t in range(4):
                o = 4 * a + t
                dhidden = jnp.dot(
                    piece_rows[64 * b : 64 * b + 64], w_down[o], preferred_element_type=F32
                ).reshape(4, 16, 128)
                for qx in range(4):
                    row = 64 * (2 * qx + a) + 16 * t
                    slopes[b, row : row + 16, :] = dhidden[qx] * factor[b, row : row + 16, :]
    arrived(piece_in.at[0 : nz - 1], front(4), partner)
    for g in range(8):
        value = piece_in[g // 2].astype(F32)
        swapped = pltpu.roll(value, 64, 1)
        first, other = (value, swapped) if g % 2 == 0 else (swapped, value)
        halves[0, g] = jnp.where(low, first, 0.0).astype(BF16)
        halves[1, g] = jnp.where(low, 0.0, other).astype(BF16)

    @pl.loop(0, peers)
    def _(d):
        place_0 = jnp.int32(8)
        place_1 = jnp.int32(8)
        for g in range(7, -1, -1):
            hit = owners[g] == d
            place_1 = jnp.where(hit, place_0, place_1)
            place_0 = jnp.where(hit, g, place_0)
        coarse_out[d] = halves[0, place_0] + halves[1, place_1]

    start_exchange(links, coarse_out, coarse_in, front(9))

    turned = [slopes[b].astype(BF16).astype(F32).T.astype(BF16) for b in range(2)]
    for dx in range(3):
        total = None
        for b in range(2):
            part = jnp.dot(
                turned[b], windows[b, dx : dx + 8].reshape(512, 1152), preferred_element_type=F32
            )
            total = part if total is None else total + part
        for d in range(9):
            k = 9 * dx + d
            color, row = CONV_ROWS[k]
            for z in range(4):
                grads[color, z, row : row + 32, :] = total[
                    32 * z : 32 * z + 32, 128 * d : 128 * d + 128
                ]
        if dx == 0:
            reduce.start_major(0)
        elif dx == 1:
            reduce.start_pair(3)
    reduce.start_pair(1)
    reduce.start_pair(2)
    reduce.start_major(3)
    reduce.start_major(1)
    reduce.start_major(2)
    for color in (0, 1, 2, 3):
        reduce.start_minor(color)
    for color in (0, 1, 2, 3):
        reduce.start_spread(color)

    arrived(coarse_in.at[0 : peers - 1], front(9), partner)

    coarse_pairs_ref[...] = coarse_in[...]
    for color in (0, 1, 2, 3):
        reduce.start_share(color)
    for color in range(4):
        reduce.finish(color)
        if color == 0:
            for o in range(8):
                down_ref[o] = sums[0, 64 * o : 64 * o + 64]
        for k in range(27):
            if CONV_ROWS[k][0] == color:
                conv_ref[k] = sums[color, CONV_ROWS[k][1] : CONV_ROWS[k][1] + 32]
    left(cot_out.at[0 : peers - 1], front(0), partner)
    left(rims.at[0, 4:8], front(1), partner)
    left(rims.at[1, 0:4], front(2), partner)
    left(piece_out.at[0 : nz - 1], front(4), partner)
    left(dpiece_out.at[0 : nz - 1], front(5), partner)
    for dx in range(3):
        left(w_conv.at[dx, 0 : 16 * (nz - 1)], front(19 + dx), partner)
        for step in range(1, nz):
            left(w_conv.at[dx, 0:16], front(10 + 3 * step + dx - 3), partner)
    left(coarse_out.at[0 : peers - 1], front(9), partner)


def finish_kernel(pairs, conv, down, coarse_out, conv_out, down_out, coarse, sems):
    quarter = pairs.shape[0] // 4
    stores = [
        pltpu.make_async_copy(conv, conv_out, sems.at[4]),
        pltpu.make_async_copy(down, down_out, sems.at[5]),
    ]
    for store in stores:
        store.start()
    for n in range(4):
        for d in range(n * quarter, (n + 1) * quarter):
            coarse[2 * d] = pairs[d, :, 0:64]
            coarse[2 * d + 1] = pairs[d, :, 64:128]
        store = pltpu.make_async_copy(
            coarse.at[2 * n * quarter : 2 * (n + 1) * quarter],
            coarse_out.at[2 * n * quarter : 2 * (n + 1) * quarter], sems.at[n],
        )
        store.start()
        stores.append(store)
    for store in stores:
        store.wait()


def local(features, voxel_mask, neighbors, w_conv, w_down, coarse_owner, cotangent):
    peers = lax.axis_size("space")
    nz = lax.axis_size("chan")
    smem = pl.BlockSpec(memory_space=pltpu.SMEM)
    vmem = pl.BlockSpec(memory_space=pltpu.VMEM)
    anywhere = pl.BlockSpec(memory_space=pl.ANY)
    coarse_pairs, conv_sum, down_sum = pl.pallas_call(
        step_kernel,
        out_shape=(
            pltpu.VMEM((peers, 64, 128), BF16),
            pltpu.VMEM((27, 32, 128), F32),
            pltpu.VMEM((8, 64, 128), F32),
        ),
        in_specs=[smem, smem] + [anywhere] * 5,
        out_specs=(vmem, vmem, vmem),
        scratch_shapes=[
            pltpu.VMEM((8, 128, 512), BF16),
            pltpu.VMEM((8, 512), jnp.int32),
            pltpu.VMEM((27, 32, 128), BF16),
            pltpu.VMEM((8, 256, 128), BF16),
            pltpu.VMEM(cotangent.shape, BF16),
            pltpu.VMEM((3, 128, 1152), BF16),
            pltpu.VMEM((65, 64, 128), BF16),
            pltpu.VMEM((2, 17, 64, 128), BF16),
            pltpu.VMEM((2, 10, 64, 1152), BF16),
            pltpu.VMEM((8, 128, 128), BF16),
            pltpu.VMEM((2, 512, 128), F32),
            pltpu.VMEM((2, 512, 128), F32),
            pltpu.VMEM((2, 512, 128), F32),
            pltpu.VMEM((peers, 64, 128), BF16),
            pltpu.VMEM((peers, 64, 128), BF16),
            pltpu.VMEM((nz, 64, 128), BF16),
            pltpu.VMEM((nz, 64, 128), BF16),
            pltpu.VMEM((nz, 64, 128), BF16),
            pltpu.VMEM((nz, 64, 128), BF16),
            pltpu.VMEM((2, 9, 64, 128), BF16),
            pltpu.VMEM((peers, 64, 128), BF16),
            pltpu.VMEM((peers, 64, 128), BF16),
            pltpu.SemaphoreType.DMA((8,)),
            pltpu.SemaphoreType.DMA((2, 22)),
        ]
        + reduce_scratch(peers, nz),
        compiler_params=pltpu.CompilerParams(
            vmem_limit_bytes=56 << 20, collective_id=0, has_side_effects=True
        ),
    )(neighbors, coarse_owner.reshape(1, 8), features, voxel_mask, w_conv, w_down, cotangent)
    return pl.pallas_call(
        finish_kernel,
        out_shape=(
            jax.ShapeDtypeStruct(cotangent.shape, BF16),
            jax.ShapeDtypeStruct((27, 32, 128), F32),
            jax.ShapeDtypeStruct((8, 64, 128), F32),
        ),
        in_specs=[vmem] * 3,
        out_specs=(anywhere,) * 3,
        scratch_shapes=[
            pltpu.VMEM(cotangent.shape, BF16), pltpu.SemaphoreType.DMA((6,)),
        ],
    )(
        *(
            pltpu.with_memory_space_constraint(value, pltpu.VMEM)
            for value in (coarse_pairs, conv_sum, down_sum)
        )
    )


def solution(mesh):
    in_specs = (
        P("space", None, None),
        P("space", None),
        P("space", None),
        P(None, "chan", None),
        P(),
        P("space", None),
        P("space", "chan", None),
    )
    out_specs = (P("space", "chan", None), P(None, "chan", None), P(None, "chan", None))
    return jax.shard_map(local, mesh=mesh, in_specs=in_specs, out_specs=out_specs, check_vma=False)
```

```python
import jax
import jax.numpy as jnp
from jax import lax
from jax.experimental import pallas as pl
from jax.experimental.pallas import tpu as pltpu
from jax.sharding import PartitionSpec as P

F32 = jnp.float32
BF16 = jnp.bfloat16
NT = (((1,), (1,)), ((), ()))


def voxel_order():
    row = lax.broadcasted_iota(jnp.int32, (256, 256), 0)
    col = lax.broadcasted_iota(jnp.int32, (256, 256), 1)
    y = ((row >> 2) & 3) * 2 + ((row >> 5) & 1)
    z = (row & 3) * 2 + ((row >> 4) & 1)
    source = (row & ~63) + y * 8 + z
    return (source == col).astype(F32).astype(BF16)


def fill_plane(windows, planes, near, b, mine, xp, sx):
    qy = (lax.broadcasted_iota(jnp.int32, (16, 128), 0) >> 2) & 3
    qz = lax.broadcasted_iota(jnp.int32, (16, 128), 0) & 3
    loaded = {}
    for sy in (-1, 0, 1):
        for sz in (-1, 0, 1):
            position = 9 * (sx + 1) + 3 * (sy + 1) + (sz + 1)
            if position == 13:
                slot = mine + b
            else:
                slot = near[mine + b, position if position < 13 else position - 1]
            if sx == 0:
                plane = jnp.where((slot < 0) | (slot > 7), 64, 8 * slot + xp - 1)
            else:
                plane = jnp.where(slot < 0, 16, slot)
            loaded[sy, sz] = planes[plane].astype(F32).reshape(4, 16, 128)

    def merged(oy, sz, tile):
        inner = loaded[0, sz][tile]
        if oy == 0:
            return inner
        return jnp.where(qy == (3 if oy < 0 else 0), loaded[oy, sz][tile], inner)

    def turned(value, shift):
        return value if shift % 16 == 0 else pltpu.roll(value, shift % 16, 0)

    for i in range(4):
        for j in range(4):
            oy = (-1, 0, 0, 1)[i]
            oz = (-1, 0, 0, 1)[j]
            tile = (1, 0, 1, 0)[i] * 2 + (1, 0, 1, 0)[j]
            value = turned(merged(oy, 0, tile), -4 * oy - oz)
            if oz != 0:
                edge = turned(merged(oy, oz, tile), -4 * oy + 3 * oz)
                value = jnp.where(qz == (0 if oz < 0 else 3), edge, value)
            value = value.astype(BF16)
            for p in range(2):
                for e in range(2):
                    dy, dz = i - p, j - e
                    if 0 <= dy <= 2 and 0 <= dz <= 2:
                        row = 32 * p + 16 * e
                        col = 128 * (3 * dy + dz)
                        windows[b, xp, row : row + 16, col : col + 128] = value


def grid_of(peers):
    chips = peers // 2
    across = 4 if chips == 16 else (2 if chips == 4 else 1)
    return chips // across, across


class Links:
    def __init__(self):
        self.ny, self.nx = grid_of(lax.axis_size("space"))
        self.nz = lax.axis_size("chan")
        space = lax.axis_index("space")
        self.space = space
        self.z = lax.axis_index("chan")
        self.core = lax.rem(space, 2)
        self.x = lax.rem(space // 2, self.nx)
        self.y = space // (2 * self.nx)

    def device(self, y=None, x=None, z=None, core=None):
        y = self.y if y is None else y
        x = self.x if x is None else x
        z = self.z if z is None else z
        core = self.core if core is None else core
        return ((y * self.nx + x) * 2 + core, z)


def send(source, target, sems, device):
    pltpu.make_async_remote_copy(
        src_ref=source, dst_ref=target, send_sem=sems[0], recv_sem=sems[1],
        device_id=device, device_id_type=pl.DeviceIdType.MESH,
    ).start()


def arrived(ref, sems, device):
    pltpu.make_async_remote_copy(
        src_ref=ref, dst_ref=ref, send_sem=sems[0], recv_sem=sems[1],
        device_id=device, device_id_type=pl.DeviceIdType.MESH,
    ).wait_recv()


def left(ref, sems, device):
    pltpu.make_async_remote_copy(
        src_ref=ref, dst_ref=ref, send_sem=sems[0], recv_sem=sems[1],
        device_id=device, device_id_type=pl.DeviceIdType.MESH,
    ).wait_send()


def shifted(place, step, count):
    return lax.rem(place + step, count)


HALF = (256, 128, 128, 256)
FULL = (256, 128, 128, 192)
LEAD = ("z", "x", "y", "z")
CONV_ROWS = [(3, 32 * k + (64 if k > 5 else 0)) for k in range(11)]
CONV_ROWS += [(1, 32 * k) for k in range(8)] + [(2, 32 * k) for k in range(8)]


def group_of(color, ny, nx, nz):
    return {
        "z": (("y", ny), ("x", nx)), "x": (("z", nz), ("y", ny)), "y": (("z", nz), ("x", nx)),
    }[LEAD[color]]


class Reduce:
    def __init__(self, links, grads, pair, first, rest, second, sums, sems):
        self.k = links
        self.grads, self.pair, self.first, self.rest = grads, pair, first, rest
        self.second, self.sums, self.sems = second, sums, sems
        self.partner = links.device(core=1 - links.core)
        k = links
        self.counts = {"z": k.nz, "x": k.nx, "y": k.ny}
        self.minor = [group_of(color, k.ny, k.nx, k.nz) for color in range(4)]
        self.cell = [half // (k.nx * k.ny) for half in HALF]

    def at(self, name):
        return getattr(self.k, name)

    def sem(self, phase, color):
        return (self.sems.at[0, phase, color], self.sems.at[1, phase, color])

    def start_pair(self, color):
        away = pl.multiple_of(HALF[color] * (1 - self.k.core), 128)
        send(
            self.grads.at[color, :, pl.ds(away, FULL[color])],
            self.pair.at[color, :, 0 : FULL[color]], self.sem(0, color), self.partner,
        )

    def part(self, color, place):
        base = HALF[color] * self.k.core
        if LEAD[color] == "z":
            return place, pl.ds(pl.multiple_of(base, 128), FULL[color])
        rows = HALF[color] // self.counts[LEAD[color]]
        return slice(None), pl.ds(pl.multiple_of(base + place * rows, rows), rows)

    def start_major(self, color):
        full = FULL[color]
        rows = pl.ds(pl.multiple_of(HALF[color] * self.k.core, 128), full)
        arrived(self.pair.at[color, :, 0:full], self.sem(0, color), self.partner)
        for z in range(self.k.nz):
            self.grads[color, z, rows] += self.pair[color, z, 0:full]
        name = LEAD[color]
        count = self.counts[name]
        for step in range(1, count):
            place = shifted(self.at(name), step, count)
            chunk, span = self.part(color, place)
            send(
                self.grads.at[color, chunk, span], self.first[color].at[step - 1],
                self.sem(1, color), self.k.device(**{name: place}),
            )

    def start_minor(self, color):
        name = LEAD[color]
        count = self.counts[name]
        if count > 1:
            arrived(self.first[color].at[0 : count - 1], self.sem(1, color), self.partner)
        chunk, span = self.part(color, self.at(name))
        total = self.grads[color, chunk, span]
        for step in range(count - 1):
            total = total + self.first[color][step]
        cell = self.cell[color]
        used = FULL[color] // cell
        if LEAD[color] != "z":
            used = self.rest[color].shape[0]
        self.rest[color][0:used] = total.reshape(used, cell, 128)
        (n0, c0), (n1, c1) = self.minor[color]
        for step0 in range(c0):
            for step1 in range(c1):
                if step0 == 0 and step1 == 0:
                    continue
                p0 = shifted(self.at(n0), step0, c0)
                p1 = shifted(self.at(n1), step1, c1)
                send(
                    self.rest[color].at[p0 * c1 + p1],
                    self.second[color].at[step0 * c1 + step1 - 1],
                    self.sem(2, color), self.k.device(**{n0: p0, n1: p1}),
                )

    def home(self, color):
        k = self.k
        inner = (k.x * k.ny + k.y) if LEAD[color] == "x" else (k.y * k.nx + k.x)
        cell = self.cell[color]
        return pl.ds(pl.multiple_of(HALF[color] * k.core + inner * cell, cell), cell)

    def start_spread(self, color):
        k = self.k
        (n0, c0), (n1, c1) = self.minor[color]
        if c0 * c1 > 1:
            arrived(self.second[color], self.sem(2, color), self.partner)
        total = self.rest[color][self.at(n0) * c1 + self.at(n1)]
        for step in range(c0 * c1 - 1):
            total = total + self.second[color][step]
        self.sums[color, self.home(color)] = total
        for step0 in range(k.ny):
            for step1 in range(k.nx):
                if step0 == 0 and step1 == 0:
                    continue
                y = shifted(k.y, step0, k.ny)
                x = shifted(k.x, step1, k.nx)
                mine = self.sums.at[color, self.home(color)]
                send(mine, mine, self.sem(3, color), k.device(y=y, x=x))

    def others(self, color):
        return self.sums.at[color, 0 : (self.k.nx * self.k.ny - 1) * self.cell[color]]

    def start_share(self, color):
        if self.k.nx * self.k.ny > 1:
            arrived(self.others(color), self.sem(3, color), self.partner)
        half = HALF[color]
        mine = self.sums.at[color, pl.ds(pl.multiple_of(half * self.k.core, 128), half)]
        send(mine, mine, self.sem(4, color), self.partner)

    def finish(self, color):
        half = self.sums.at[color, 0 : HALF[color]]
        arrived(half, self.sem(4, color), self.partner)
        left(self.pair.at[color, :, 0 : FULL[color]], self.sem(0, color), self.partner)
        count = self.counts[LEAD[color]]
        if count > 1:
            left(self.first[color].at[0 : count - 1], self.sem(1, color), self.partner)
        if self.minor[color][0][1] * self.minor[color][1][1] > 1:
            left(self.second[color], self.sem(2, color), self.partner)
        if self.k.nx * self.k.ny > 1:
            left(self.others(color), self.sem(3, color), self.partner)
        left(half, self.sem(4, color), self.partner)


def reduce_scratch(peers, nz):
    ny, nx = grid_of(peers)
    counts = {"z": nz, "x": nx, "y": ny}
    first, rest, second = [], [], []
    for color in range(4):
        count = counts[LEAD[color]]
        if LEAD[color] == "z":
            shape = (max(count - 1, 1), FULL[color], 128)
        else:
            shape = (max(count - 1, 1), nz, HALF[color] // count, 128)
        first.append(pltpu.VMEM(shape, F32))
        (_, c0), (_, c1) = group_of(color, ny, nx, nz)
        cell = HALF[color] // (nx * ny)
        rest.append(pltpu.VMEM((c0 * c1, cell, 128), F32))
        second.append(pltpu.VMEM((max(c0 * c1 - 1, 1), cell, 128), F32))
    return [
        pltpu.VMEM((4, nz, 512, 128), F32), pltpu.VMEM((4, nz, 256, 128), F32),
        *first, *rest, *second,
        pltpu.VMEM((4, 512, 128), F32), pltpu.SemaphoreType.DMA((2, 5, 4)),
    ]


def signal_all(links):
    barrier = pltpu.get_barrier_semaphore()
    k = links
    targets = []
    for step in range(1, k.nz):
        z = shifted(k.z, step, k.nz)
        for other in range(k.ny):
            targets.append(k.device(y=shifted(k.y, other, k.ny), z=z))
        for other in range(1, k.nx):
            targets.append(k.device(x=shifted(k.x, other, k.nx), z=z))
    for step in range(1, k.ny * k.nx * 2):
        targets.append((shifted(k.space, step, k.ny * k.nx * 2), k.z))
    for target in targets:
        pl.semaphore_signal(
            barrier, inc=1, device_id=target, device_id_type=pl.DeviceIdType.MESH
        )
    return barrier, len(targets)


def start_exchange(links, source, target, sems):
    peers = links.ny * links.nx * 2
    for step in range(1, peers):
        place = shifted(links.space, step, peers)
        send(source.at[place], target.at[links.space], sems, (place, links.z))
    target[links.space] = source[links.space]


def start_columns(links, source, target, sems):
    for step in range(1, links.nz):
        place = shifted(links.z, step, links.nz)
        send(source.at[place], target.at[links.z], sems, (links.space, place))
    target[links.z] = source[links.z]


def step_kernel(
    near, owner, features_hbm, mask_hbm, w_conv_hbm, w_down_hbm, cotangent_hbm,
    coarse_pairs_ref, conv_ref, down_ref,
    features, mask, w_own, w_down, cotangent, w_conv,
    table, rims, windows, octants, factor, slopes, row_mask,
    cot_out, cot_in, piece_out, piece_in, dpiece_out, dpiece_in,
    halves, coarse_out, coarse_in, local_sems, front_sems,
    grads, pair, first_0, first_1, first_2, first_3, rest_0, rest_1, rest_2, rest_3,
    second_0, second_1, second_2, second_3, sums, sems,
):
    links = Links()
    peers = links.ny * links.nx * 2
    nz = links.nz
    partner = links.device(core=1 - links.core)
    mine = links.z * 2
    reduce = Reduce(
        links, grads, pair, (first_0, first_1, first_2, first_3),
        (rest_0, rest_1, rest_2, rest_3), (second_0, second_1, second_2, second_3), sums, sems,
    )

    def front(n):
        return (front_sems.at[0, n], front_sems.at[1, n])

    def pass_on(dx):
        for step in range(1, nz):
            z = shifted(links.z, nz - step, nz)
            rows = pl.ds(pl.multiple_of(32 * z + 16 * links.core, 16), 16)
            piece = w_conv.at[dx, rows]
            arrived(piece, front(10 + 3 * step + dx - 3), partner)
            send(piece, piece, front(19 + dx), partner)

    loads = [
        pltpu.make_async_copy(source, target, local_sems.at[n])
        for n, (source, target) in enumerate(
            (
                (w_conv_hbm, w_own), (cotangent_hbm, cotangent), (mask_hbm, mask),
                (features_hbm, features), (w_down_hbm, w_down),
            )
        )
    ]
    for load in loads:
        load.start()
    barrier, signals = signal_all(links)
    order = voxel_order()

    table[64] = jnp.zeros((64, 128), BF16)
    rims[0, 12:17] = jnp.zeros((5, 64, 128), BF16)
    rims[1, 8:12] = jnp.zeros((4, 64, 128), BF16)
    rims[1, 16] = jnp.zeros((64, 128), BF16)
    for z in range(nz):
        grads[3, z, 416:448] = jnp.zeros((32, 128), F32)
    rest_3[...] = jnp.zeros_like(rest_3)
    for r in range(2):
        halves[r, 8] = jnp.zeros((64, 128), BF16)
    loads[0].wait()
    for k in range(27):
        dx, d = k // 9, k % 9
        rows = pl.ds(pl.multiple_of(32 * links.z, 32), 32)
        w_conv[dx, rows, 128 * d : 128 * d + 128] = w_own[k]
    loads[1].wait()

    @pl.loop(0, peers)
    def _(d):
        cot_out[d, :, 0:64] = cotangent[2 * d]
        cot_out[d, :, 64:128] = cotangent[2 * d + 1]

    loads[2].wait()
    loads[3].wait()

    @pl.loop(0, 4)
    def _(g):
        keep = mask[pl.ds(g, 1), :].astype(F32).astype(BF16)
        masked = features[g] * keep
        for h in range(2):
            turned = lax.dot_general(
                order, masked[:, 256 * h : 256 * h + 256], NT, preferred_element_type=F32
            )
            table[pl.ds(8 * g + 4 * h, 4)] = turned.astype(BF16).reshape(4, 64, 128)

    pl.semaphore_wait(barrier, signals)
    own_rows = pl.ds(pl.multiple_of(32 * links.z + 16 * links.core, 16), 16)
    for dx in range(3):
        for step in range(1, nz):
            z = shifted(links.z, step, nz)
            piece = w_conv.at[dx, own_rows]
            send(piece, piece, front(10 + 3 * step + dx - 3), links.device(z=z))


    @pl.loop(4, 8)
    def _(g):
        keep = mask[pl.ds(g, 1), :].astype(F32).astype(BF16)
        masked = features[g] * keep
        for h in range(2):
            turned = lax.dot_general(
                order, masked[:, 256 * h : 256 * h + 256], NT, preferred_element_type=F32
            )
            table[pl.ds(8 * g + 4 * h, 4)] = turned.astype(BF16).reshape(4, 64, 128)

    following = (shifted(links.space, 1, peers), links.z)
    previous = (shifted(links.space, peers - 1, peers), links.z)
    for j in range(8):
        rims[0, j] = table[8 * j + 7]
        rims[1, j] = table[8 * j]
    send(rims.at[0, 4:8], rims.at[0, 8:12], front(1), following)
    send(rims.at[1, 0:4], rims.at[1, 12:16], front(2), previous)
    start_exchange(links, cot_out, cot_in, front(0))
    for b in range(2):
        keep = mask[pl.ds(mine + b, 1), :].astype(F32)
        for h in range(2):
            wide = jnp.broadcast_to(keep[:, 256 * h : 256 * h + 256], (128, 256)).astype(BF16)
            turned = lax.dot_general(order, wide, NT, preferred_element_type=F32)
            row_mask[b, 256 * h : 256 * h + 256, :] = turned

        @pl.loop(1, 9)
        def _(xp):
            fill_plane(windows, table, near, b, mine, xp, 0)

    pass_on(0)
    arrived(rims.at[0, 8:12], front(1), previous)
    arrived(rims.at[1, 12:16], front(2), following)

    @pl.when(links.space == 0)
    def _():
        rims[0, 8:12] = jnp.zeros((4, 64, 128), BF16)

    @pl.when(links.space == peers - 1)
    def _():
        rims[1, 12:16] = jnp.zeros((4, 64, 128), BF16)

    for b in range(2):
        fill_plane(windows, rims.at[0], near, b, mine, 0, -1)
        fill_plane(windows, rims.at[1], near, b, mine, 9, 1)
    for dx in range(3):
        if dx < 2:
            pass_on(dx + 1)
        else:
            arrived(cot_in.at[0 : peers - 1], front(0), partner)
            owners = [owner[0, g] for g in range(8)]
            low = lax.broadcasted_iota(jnp.int32, (64, 128), 1) < 64
            for z in range(4):
                parts = []
                for i in range(2):
                    g = 2 * z + i
                    rank = jnp.int32(0)
                    for h in range(g):
                        rank = rank + jnp.where(owners[h] == owners[g], 1, 0)
                    value = cot_in[owners[g]].astype(F32)
                    parts.append(jnp.where(rank == i, value, pltpu.roll(value, 64, 1)))
                dpiece_out[z] = jnp.where(low, parts[0], parts[1]).astype(BF16)
            start_columns(links, dpiece_out, dpiece_in, front(5))

        arrived(w_conv.at[dx, 0 : 16 * (nz - 1)], front(19 + dx), partner)
        for b in range(2):
            part = lax.dot_general(
                windows[b, dx : dx + 8].reshape(512, 1152), w_conv[dx], NT,
                preferred_element_type=F32,
            )
            if dx == 0:
                slopes[b] = part
            else:
                slopes[b] += part
    for b in range(2):
        own = table[pl.ds(8 * (mine + b), 8)].astype(F32).reshape(512, 128)
        pre = own + slopes[b]
        keep = row_mask[b]
        gate = jax.nn.sigmoid(pre)
        hidden = (keep * (pre * gate)).astype(BF16).reshape(4, 2, 4, 16, 128)
        factor[b] = keep * gate * (1.0 + pre * (1.0 - gate))
        for a in range(2):
            for t in range(4):
                octants[4 * a + t, 64 * b : 64 * b + 64, :] = hidden[:, a, t].reshape(64, 128)
    loads[4].wait()
    total = None
    for o in range(8):
        part = lax.dot_general(w_down[o], octants[o], NT, preferred_element_type=F32)
        total = part if total is None else total + part
    piece_out[...] = total.astype(BF16).reshape(nz, 64, 128)
    start_columns(links, piece_out, piece_in, front(4))

    arrived(dpiece_in.at[0 : nz - 1], front(5), partner)
    piece = dpiece_in[...].reshape(256, 128)
    piece_rows = piece.astype(F32).T.astype(BF16)
    for b in range(2):
        for a in range(2):
            for t in range(4):
                o = 4 * a + t
                dhidden = jnp.dot(
                    piece_rows[64 * b : 64 * b + 64], w_down[o], preferred_element_type=F32
                ).reshape(4, 16, 128)
                for qx in range(4):
                    row = 64 * (2 * qx + a) + 16 * t
                    slopes[b, row : row + 16, :] = dhidden[qx] * factor[b, row : row + 16, :]
    for o in range(8):
        part = jnp.dot(piece, octants[o], preferred_element_type=F32)
        for z in range(4):
            grads[0, z, 64 * o : 64 * o + 64, :] = part[64 * z : 64 * z + 64]
    reduce.start_pair(0)
    arrived(piece_in.at[0 : nz - 1], front(4), partner)
    for g in range(8):
        value = piece_in[g // 2].astype(F32)
        swapped = pltpu.roll(value, 64, 1)
        first, other = (value, swapped) if g % 2 == 0 else (swapped, value)
        halves[0, g] = jnp.where(low, first, 0.0).astype(BF16)
        halves[1, g] = jnp.where(low, 0.0, other).astype(BF16)

    @pl.loop(0, peers)
    def _(d):
        place_0 = jnp.int32(8)
        place_1 = jnp.int32(8)
        for g in range(7, -1, -1):
            hit = owners[g] == d
            place_1 = jnp.where(hit, place_0, place_1)
            place_0 = jnp.where(hit, g, place_0)
        coarse_out[d] = halves[0, place_0] + halves[1, place_1]

    start_exchange(links, coarse_out, coarse_in, front(9))

    turned = [slopes[b].astype(BF16).astype(F32).T.astype(BF16) for b in range(2)]
    for dx in range(3):
        total = None
        for b in range(2):
            part = jnp.dot(
                turned[b], windows[b, dx : dx + 8].reshape(512, 1152), preferred_element_type=F32
            )
            total = part if total is None else total + part
        for d in range(9):
            k = 9 * dx + d
            color, row = CONV_ROWS[k]
            for z in range(4):
                grads[color, z, row : row + 32, :] = total[
                    32 * z : 32 * z + 32, 128 * d : 128 * d + 128
                ]
        if dx == 0:
            reduce.start_major(0)
        elif dx == 1:
            reduce.start_pair(3)
    reduce.start_pair(1)
    reduce.start_pair(2)
    reduce.start_major(3)
    reduce.start_major(1)
    reduce.start_major(2)
    for color in (0, 1, 2, 3):
        reduce.start_minor(color)
    for color in (0, 1, 2, 3):
        reduce.start_spread(color)

    arrived(coarse_in.at[0 : peers - 1], front(9), partner)

    coarse_pairs_ref[...] = coarse_in[...]
    for color in (0, 1, 2, 3):
        reduce.start_share(color)
    for color in range(4):
        reduce.finish(color)
        if color == 0:
            for o in range(8):
                down_ref[o] = sums[0, 64 * o : 64 * o + 64]
        for k in range(27):
            if CONV_ROWS[k][0] == color:
                conv_ref[k] = sums[color, CONV_ROWS[k][1] : CONV_ROWS[k][1] + 32]
    left(cot_out.at[0 : peers - 1], front(0), partner)
    left(rims.at[0, 4:8], front(1), partner)
    left(rims.at[1, 0:4], front(2), partner)
    left(piece_out.at[0 : nz - 1], front(4), partner)
    left(dpiece_out.at[0 : nz - 1], front(5), partner)
    for dx in range(3):
        left(w_conv.at[dx, 0 : 16 * (nz - 1)], front(19 + dx), partner)
        for step in range(1, nz):
            left(w_conv.at[dx, 0:16], front(10 + 3 * step + dx - 3), partner)
    left(coarse_out.at[0 : peers - 1], front(9), partner)


def finish_kernel(pairs, conv, down, coarse_out, conv_out, down_out, coarse, sems):
    quarter = pairs.shape[0] // 4
    stores = [
        pltpu.make_async_copy(conv, conv_out, sems.at[4]),
        pltpu.make_async_copy(down, down_out, sems.at[5]),
    ]
    for store in stores:
        store.start()
    for n in range(4):
        for d in range(n * quarter, (n + 1) * quarter):
            coarse[2 * d] = pairs[d, :, 0:64]
            coarse[2 * d + 1] = pairs[d, :, 64:128]
        store = pltpu.make_async_copy(
            coarse.at[2 * n * quarter : 2 * (n + 1) * quarter],
            coarse_out.at[2 * n * quarter : 2 * (n + 1) * quarter], sems.at[n],
        )
        store.start()
        stores.append(store)
    for store in stores:
        store.wait()


def local(features, voxel_mask, neighbors, w_conv, w_down, coarse_owner, cotangent):
    peers = lax.axis_size("space")
    nz = lax.axis_size("chan")
    smem = pl.BlockSpec(memory_space=pltpu.SMEM)
    vmem = pl.BlockSpec(memory_space=pltpu.VMEM)
    anywhere = pl.BlockSpec(memory_space=pl.ANY)
    coarse_pairs, conv_sum, down_sum = pl.pallas_call(
        step_kernel,
        out_shape=(
            pltpu.VMEM((peers, 64, 128), BF16),
            pltpu.VMEM((27, 32, 128), F32),
            pltpu.VMEM((8, 64, 128), F32),
        ),
        in_specs=[smem, smem] + [anywhere] * 5,
        out_specs=(vmem, vmem, vmem),
        scratch_shapes=[
            pltpu.VMEM((8, 128, 512), BF16),
            pltpu.VMEM((8, 512), jnp.int32),
            pltpu.VMEM((27, 32, 128), BF16),
            pltpu.VMEM((8, 256, 128), BF16),
            pltpu.VMEM(cotangent.shape, BF16),
            pltpu.VMEM((3, 128, 1152), BF16),
            pltpu.VMEM((65, 64, 128), BF16),
            pltpu.VMEM((2, 17, 64, 128), BF16),
            pltpu.VMEM((2, 10, 64, 1152), BF16),
            pltpu.VMEM((8, 128, 128), BF16),
            pltpu.VMEM((2, 512, 128), F32),
            pltpu.VMEM((2, 512, 128), F32),
            pltpu.VMEM((2, 512, 128), F32),
            pltpu.VMEM((peers, 64, 128), BF16),
            pltpu.VMEM((peers, 64, 128), BF16),
            pltpu.VMEM((nz, 64, 128), BF16),
            pltpu.VMEM((nz, 64, 128), BF16),
            pltpu.VMEM((nz, 64, 128), BF16),
            pltpu.VMEM((nz, 64, 128), BF16),
            pltpu.VMEM((2, 9, 64, 128), BF16),
            pltpu.VMEM((peers, 64, 128), BF16),
            pltpu.VMEM((peers, 64, 128), BF16),
            pltpu.SemaphoreType.DMA((8,)),
            pltpu.SemaphoreType.DMA((2, 22)),
        ]
        + reduce_scratch(peers, nz),
        compiler_params=pltpu.CompilerParams(
            vmem_limit_bytes=56 << 20, collective_id=0, has_side_effects=True
        ),
    )(neighbors, coarse_owner.reshape(1, 8), features, voxel_mask, w_conv, w_down, cotangent)
    return pl.pallas_call(
        finish_kernel,
        out_shape=(
            jax.ShapeDtypeStruct(cotangent.shape, BF16),
            jax.ShapeDtypeStruct((27, 32, 128), F32),
            jax.ShapeDtypeStruct((8, 64, 128), F32),
        ),
        in_specs=[vmem] * 3,
        out_specs=(anywhere,) * 3,
        scratch_shapes=[
            pltpu.VMEM(cotangent.shape, BF16), pltpu.SemaphoreType.DMA((6,)),
        ],
    )(
        *(
            pltpu.with_memory_space_constraint(value, pltpu.VMEM)
            for value in (coarse_pairs, conv_sum, down_sum)
        )
    )


def solution(mesh):
    in_specs = (
        P("space", None, None),
        P("space", None),
        P("space", None),
        P(None, "chan", None),
        P(),
        P("space", None),
        P("space", "chan", None),
    )
    out_specs = (P("space", "chan", None), P(None, "chan", None), P(None, "chan", None))
    return jax.shard_map(local, mesh=mesh, in_specs=in_specs, out_specs=out_specs, check_vma=False)
```
